512 devices in a mesh: ctx: 128 (over z, x_hi, y), tp: 4 (over x_lo, core).
Axes of the slice: x: 4 (x_hi: 2, x_lo: 2; x = x_hi * 2 + x_lo), y: 4, z: 16, core: 2. Of those that a mesh axis runs over, the one named last changes fastest.
Arguments:
- streams: bfloat16 [3, 256, 16384], P(None, 'tp', 'ctx'), may hold values from -6 to 6
- filter_raw: float32 [256, 16384], P('tp', 'ctx'), may hold values from -6 to 6
- grad_output: bfloat16 [256, 16384], P('tp', 'ctx'), may hold values from -6 to 6
Outputs:
- mixed_out: bfloat16 [256, 16384], P('tp', 'ctx')
- grad_streams: bfloat16 [3, 256, 16384], P(None, 'tp', 'ctx')
- grad_filter: float32 [256, 16384], P('tp', 'ctx')
The draws below stay inside these ranges and needn't reach their ends.
All inputs are finite; a program needn't handle non-finite values.
Results may differ from the reference program's by a relative error of at most 0.0014.
Values sent between devices are 32-bit elements; how exact they have to be, the bound alone decides.
A program may use at most 64 MiB of HBM per device.

```python
import jax
import jax.numpy as jnp

SLAB = 256
TOKENS = 16384


def level_of(rng, dims, pieces, low, largest):
    def one(axis_at, shards_of):
        heights = jax.random.uniform(jax.random.fold_in(jax.random.fold_in(rng, 6), axis_at), (shards_of,), jnp.float32, low / len(pieces), largest / len(pieces))
        return jnp.repeat(jnp.exp(heights), dims[axis_at] // shards_of).reshape((-1,) + (1,) * (len(dims) - axis_at - 1))

    level = one(*pieces[0])
    for cut in pieces[1:]:
        level = level * one(*cut)
    return level


def scatter_about(own_key, extent, width, reach, cuts=(), kind=jnp.bfloat16):
    values = jax.random.normal(own_key, extent, jnp.float32) * width
    if len(cuts) > 0:
        values = level_of(own_key, extent, cuts, -0.22, 0.18) * values
    return jnp.clip(values, min=-reach, max=reach).astype(kind)


def setup_inputs(seed: int = 0) -> dict:
    streams_of = jax.random.split(jax.random.key(seed), 4)
    streams = scatter_about(streams_of[0], (3, SLAB, TOKENS), 1.0, 6.0, ((1, 4), (2, 128)))
    filter_raw = scatter_about(streams_of[1], (SLAB, TOKENS), 1.0, 6.0, ((0, 4), (1, 128)), jnp.float32)
    grad_output = scatter_about(streams_of[2], (SLAB, TOKENS), 1.0, 6.0, ((0, 4), (1, 128)))
    return {"streams": streams, "filter_raw": filter_raw, "grad_output": grad_output}


def reference(streams, filter_raw, grad_output):
    query_part = streams[0].astype(jnp.float32)
    key_part = streams[1].astype(jnp.float32)
    value_part = streams[2].astype(jnp.float32)
    gated_input = key_part * value_part
    tap_scale = 1.0 / TOKENS ** 0.5
    kernel_taps = filter_raw.astype(jnp.float32) * tap_scale
    length = 2 * TOKENS
    spec_gated = jnp.fft.rfft(gated_input, n=length, axis=1)
    spec_taps = jnp.fft.rfft(kernel_taps, n=length, axis=1)
    long_conv = jnp.fft.irfft(spec_gated * spec_taps, n=length, axis=1)[:, :TOKENS]
    mixed_out = (query_part * long_conv).astype(jnp.bfloat16)
    upstream = grad_output.astype(jnp.float32)
    grad_conv = query_part * upstream
    grad_query = (upstream * long_conv).astype(jnp.bfloat16)
    spec_grad = jnp.fft.rfft(grad_conv, n=length, axis=1)
    grad_gated = jnp.fft.irfft(spec_grad * jnp.conj(spec_taps), n=length, axis=1)[:, :TOKENS]
    grad_filter = jnp.fft.irfft(spec_grad * jnp.conj(spec_gated), n=length, axis=1)[:, :TOKENS] * tap_scale
    grad_key = (grad_gated * value_part).astype(jnp.bfloat16)
    grad_value = (grad_gated * key_part).astype(jnp.bfloat16)
    grad_streams = jnp.stack([grad_query, grad_key, grad_value], axis=0)
    return mixed_out, grad_streams, grad_filter.astype(jnp.float32)
```

```python
import math

import jax
import jax.numpy as jnp
import numpy as np
from jax import lax
from jax.experimental import pallas as pl
from jax.experimental.pallas import tpu as pltpu
from jax.sharding import PartitionSpec as P

MESH = pl.DeviceIdType.MESH
BARRIER = "full"


def split_table(table):
    high = table.astype(jnp.bfloat16)
    low = (table - high.astype(np.float64)).astype(jnp.bfloat16)
    return high, low


def make_tables(rows, lanes):
    length = 2 * rows * lanes
    place = np.arange(rows, dtype=np.int64)
    twice = 2 * np.arange(rows, dtype=np.int64) + 1
    column = np.arange(lanes, dtype=np.int64)
    angle = 2.0 * np.pi / (4 * rows) * (twice[:, None] * place[None, :] % (4 * rows))
    outer = np.concatenate([np.cos(angle), -np.sin(angle)], axis=0)
    angle = 2.0 * np.pi / lanes * (column[:, None] * column[None, :] % lanes)
    cosine, sine = np.cos(angle), np.sin(angle)
    inner = np.block([[cosine, -sine], [sine, cosine]])
    angle = 2.0 * np.pi / (2 * length) * (twice[:, None] * column[None, :] % (2 * length))
    twist = np.stack([np.cos(angle), np.sin(angle)]).astype(np.float32)
    scale = 2.0 / length
    tables = []
    for table in (outer, inner, inner.T, outer.T * scale):
        tables.extend(split_table(table))
    return tables + [twist]


def split_value(value):
    high = value.astype(jnp.bfloat16)
    low = (value - high.astype(jnp.float32)).astype(jnp.bfloat16)
    return high, low


def dot(left, right):
    return jnp.dot(left, right, preferred_element_type=jnp.float32)


def table_times(high, low, value):
    value_high, value_low = split_value(value)
    return dot(high[...], value_high) + (dot(high[...], value_low) + dot(low[...], value_high))


def times_table(value, high, low):
    value_high, value_low = split_value(value)
    return dot(value_high, high[...]) + (dot(value_low, high[...]) + dot(value_high, low[...]))


def far_first(step, count):
    half = count // 2
    back = (step + 1) // 2
    return lax.select(lax.rem(step, 2) == 0, half - back, half + back)


def kernel(
    devices,
    tap_scale,
    streams_ref,
    filter_ref,
    grad_ref,
    *refs,
):
    tables_hbm = refs[:9]
    mixed_ref, grads_ref, taps_ref = refs[9:12]
    outgoing, arrived, results, returned = refs[12:16]
    tables = refs[16:25]
    (table_sem, out_send, out_recv, back_send, back_recv, self_sem) = refs[25:]
    channels, lanes = filter_ref.shape
    me = lax.axis_index("ctx")
    tp = lax.axis_index("tp")
    spread = devices // channels
    core = lax.rem(tp, spread)
    mine = me // spread
    owner = lax.rem(me, spread) == core

    barrier = pltpu.get_barrier_semaphore()

    @pl.loop(1, devices)
    def _(step):
        peer = lax.rem(me + step, devices)
        pl.semaphore_signal(barrier, inc=1, device_id=(peer, tp), device_id_type=MESH)

    loads = [
        pltpu.make_async_copy(source, target, table_sem.at[at])
        for at, (source, target) in enumerate(zip(tables_hbm, tables))
    ]
    for load in loads:
        load.start()

    query = streams_ref[0].astype(jnp.float32)
    key = streams_ref[1].astype(jnp.float32)
    value = streams_ref[2].astype(jnp.float32)
    upstream = grad_ref[...].astype(jnp.float32)
    outgoing[:, 0, 0:lanes] = key * value
    outgoing[:, 0, lanes : 2 * lanes] = filter_ref[...] * tap_scale
    outgoing[:, 0, 2 * lanes : 3 * lanes] = query * upstream

    pl.semaphore_wait(barrier, devices - 1)

    def send_out(channel):
        return pltpu.make_async_remote_copy(
            src_ref=outgoing.at[channel],
            dst_ref=arrived.at[me],
            send_sem=out_send,
            recv_sem=out_recv,
            device_id=(channel * spread + core, tp),
            device_id_type=MESH,
        )

    def keep(source, target):
        return pltpu.make_async_copy(source, target, self_sem)

    @pl.loop(0, channels - 1)
    def _(step):
        send_out(lax.rem(mine + far_first(step, channels), channels)).start()

    @pl.when(jnp.logical_not(owner))
    def _():
        send_out(mine).start()

    @pl.when(owner)
    def _():
        keep(outgoing.at[mine], arrived.at[me]).start()
        keep(outgoing.at[mine], arrived.at[me]).wait()

    for load in loads:
        load.wait()

    outer_high, outer_low, inner_high, inner_low = tables[:4]
    back_high, back_low, final_high, final_low, twist = tables[4:]

    def send_back(target):
        return pltpu.make_async_remote_copy(
            src_ref=results.at[target],
            dst_ref=returned.at[mine],
            send_sem=back_send,
            recv_sem=back_recv,
            device_id=(target, tp),
            device_id_type=MESH,
        )

    def block_copy(block, send_sem, recv_sem):
        return pltpu.make_async_remote_copy(
            src_ref=block,
            dst_ref=block,
            send_sem=send_sem,
            recv_sem=recv_sem,
            device_id=(lax.rem(me + 1, devices), tp),
            device_id_type=MESH,
        )

    @pl.when(owner)
    def _():
        block_copy(arrived.at[pl.ds(0, devices - 1)], out_send, out_recv).wait_recv()
        cosine, sine = twist[0], twist[1]
        signal = jnp.concatenate(
            [arrived[:, 0, at * lanes : (at + 1) * lanes] for at in range(3)], axis=1
        )
        rows = table_times(outer_high, outer_low, signal)
        spectra = []
        for at in range(3):
            real = rows[:devices, at * lanes : (at + 1) * lanes]
            imag = rows[devices:, at * lanes : (at + 1) * lanes]
            turned = jnp.concatenate(
                [real * cosine + imag * sine, imag * cosine - real * sine], axis=1
            )
            both = times_table(turned, inner_high, inner_low)
            spectra.append((both[:, :lanes], both[:, lanes:]))
        (gated_r, gated_i), (taps_r, taps_i), (grad_r, grad_i) = spectra
        products = (
            (gated_r * taps_r - gated_i * taps_i, gated_r * taps_i + gated_i * taps_r),
            (grad_r * taps_r + grad_i * taps_i, grad_i * taps_r - grad_r * taps_i),
            (grad_r * gated_r + grad_i * gated_i, grad_i * gated_r - grad_r * gated_i),
        )
        columns = []
        for real, imag in products:
            both = times_table(jnp.concatenate([real, imag], axis=1), back_high, back_low)
            real, imag = both[:, :lanes], both[:, lanes:]
            columns.append(
                jnp.concatenate([real * cosine - imag * sine, imag * cosine + real * sine], axis=0)
            )
        final = table_times(final_high, final_low, jnp.concatenate(columns, axis=1))
        for at in range(3):
            results[:, 0, at * lanes : (at + 1) * lanes] = final[:, at * lanes : (at + 1) * lanes]

        @pl.loop(0, devices - 1)
        def _(step):
            send_back(lax.rem(me + far_first(step, devices), devices)).start()

        keep(results.at[me], returned.at[mine]).start()
        keep(results.at[me], returned.at[mine]).wait()
        block_copy(returned.at[pl.ds(0, channels - 1)], back_send, back_recv).wait_recv()
        block_copy(outgoing.at[pl.ds(0, channels - 1)], out_send, out_recv).wait_send()

    @pl.when(jnp.logical_not(owner))
    def _():
        block_copy(returned, back_send, back_recv).wait_recv()
        block_copy(outgoing, out_send, out_recv).wait_send()

    long_conv = returned[:, 0, 0:lanes]
    grad_gated = returned[:, 0, lanes : 2 * lanes]
    mixed_ref[...] = (streams_ref[0].astype(jnp.float32) * long_conv).astype(jnp.bfloat16)
    grads_ref[0] = (grad_ref[...].astype(jnp.float32) * long_conv).astype(jnp.bfloat16)
    grads_ref[1] = (grad_gated * streams_ref[2].astype(jnp.float32)).astype(jnp.bfloat16)
    grads_ref[2] = (grad_gated * streams_ref[1].astype(jnp.float32)).astype(jnp.bfloat16)
    taps_ref[...] = returned[:, 0, 2 * lanes : 3 * lanes] * tap_scale

    @pl.when(owner)
    def _():
        block_copy(results.at[pl.ds(0, devices - 1)], back_send, back_recv).wait_send()


def local(devices, streams, filter_raw, grad_output):
    channels, lanes = filter_raw.shape
    tap_scale = 1.0 / math.sqrt(lanes * devices)
    tables = [jnp.asarray(table) for table in make_tables(devices, lanes)]
    vmem = pl.BlockSpec(memory_space=pltpu.VMEM)
    hbm = pl.BlockSpec(memory_space=pl.ANY)
    width = 3 * lanes
    import functools

    return pl.pallas_call(
        functools.partial(kernel, devices, tap_scale),
        out_shape=(
            jax.ShapeDtypeStruct((channels, lanes), jnp.bfloat16),
            jax.ShapeDtypeStruct((3, channels, lanes), jnp.bfloat16),
            jax.ShapeDtypeStruct((channels, lanes), jnp.float32),
        ),
        in_specs=[vmem] * 3 + [hbm] * len(tables),
        out_specs=(vmem, vmem, vmem),
        scratch_shapes=[
            pltpu.VMEM((channels, 1, width), jnp.float32),
            pltpu.VMEM((devices, 1, width), jnp.float32),
            pltpu.VMEM((devices, 1, width), jnp.float32),
            pltpu.VMEM((channels, 1, width), jnp.float32),
        ]
        + [pltpu.VMEM(table.shape, table.dtype) for table in tables]
        + [pltpu.SemaphoreType.DMA((len(tables),))]
        + [pltpu.SemaphoreType.DMA] * 5,
        compiler_params=pltpu.CompilerParams(
            collective_id=0, has_side_effects=True, vmem_limit_bytes=32 << 20
        ),
    )(streams, filter_raw, grad_output, *tables)


def solution(mesh):
    devices = mesh.shape["ctx"]
    in_specs = (P(None, "tp", "ctx"), P("tp", "ctx"), P("tp", "ctx"))
    out_specs = (P("tp", "ctx"), P(None, "tp", "ctx"), P("tp", "ctx"))

    def program(streams, filter_raw, grad_output):
        return local(devices, streams, filter_raw, grad_output)

    return jax.shard_map(
        program, mesh=mesh, in_specs=in_specs, out_specs=out_specs, check_vma=False
    )
```

```python
import functools
import math

import jax
import jax.numpy as jnp
import numpy as np
from jax import lax
from jax.experimental import pallas as pl
from jax.experimental.pallas import tpu as pltpu
from jax.sharding import PartitionSpec as P

MESH = pl.DeviceIdType.MESH
ACROSS = 4
FIRST = 4


def split_table(table):
    high = table.astype(jnp.bfloat16)
    low = (table - high.astype(np.float64)).astype(jnp.bfloat16)
    return high, low


def make_tables(rows, lanes):
    length = 2 * rows * lanes
    place = np.arange(rows, dtype=np.int64)
    twice = 2 * np.arange(rows, dtype=np.int64) + 1
    column = np.arange(lanes, dtype=np.int64)
    angle = 2.0 * np.pi / (4 * rows) * (twice[:, None] * place[None, :] % (4 * rows))
    outer = np.concatenate([np.cos(angle), -np.sin(angle)], axis=0)
    angle = 2.0 * np.pi / lanes * (column[:, None] * column[None, :] % lanes)
    cosine, sine = np.cos(angle), np.sin(angle)
    inner = np.block([[cosine, -sine], [sine, cosine]])
    angle = 2.0 * np.pi / (2 * length) * (twice[:, None] * column[None, :] % (2 * length))
    twist = np.stack([np.cos(angle), np.sin(angle)]).astype(np.float32)
    scale = 2.0 / length
    tables = []
    for table in (outer, inner, inner.T, outer.T * scale):
        tables.extend(split_table(table))
    return tables + [twist]


def split_value(value):
    high = value.astype(jnp.bfloat16)
    low = (value - high.astype(jnp.float32)).astype(jnp.bfloat16)
    return high, low


def dot(left, right):
    return jnp.dot(left, right, preferred_element_type=jnp.float32)


def table_times(high, low, value):
    value_high, value_low = split_value(value)
    return dot(high[...], value_high) + (dot(high[...], value_low) + dot(low[...], value_high))


def times_table(value, high, low):
    value_high, value_low = split_value(value)
    return dot(value_high, high[...]) + (dot(value_low, high[...]) + dot(value_high, low[...]))


def convolve(signal, tables, rows_count, lanes):
    outer_high, outer_low, inner_high, inner_low = tables[:4]
    back_high, back_low, final_high, final_low, twist = tables[4:]
    cosine, sine = twist[0], twist[1]
    rows = table_times(outer_high, outer_low, signal)
    spectra = []
    for at in range(3):
        real = rows[:rows_count, at * lanes : (at + 1) * lanes]
        imag = rows[rows_count:, at * lanes : (at + 1) * lanes]
        turned = jnp.concatenate([real * cosine + imag * sine, imag * cosine - real * sine], axis=1)
        both = times_table(turned, inner_high, inner_low)
        spectra.append((both[:, :lanes], both[:, lanes:]))
    (gated_r, gated_i), (taps_r, taps_i), (grad_r, grad_i) = spectra
    products = (
        (gated_r * taps_r - gated_i * taps_i, gated_r * taps_i + gated_i * taps_r),
        (grad_r * taps_r + grad_i * taps_i, grad_i * taps_r - grad_r * taps_i),
        (grad_r * gated_r + grad_i * gated_i, grad_i * gated_r - grad_r * gated_i),
    )
    columns = []
    for real, imag in products:
        both = times_table(jnp.concatenate([real, imag], axis=1), back_high, back_low)
        real, imag = both[:, :lanes], both[:, lanes:]
        columns.append(
            jnp.concatenate([real * cosine - imag * sine, imag * cosine + real * sine], axis=0)
        )
    return table_times(final_high, final_low, jnp.concatenate(columns, axis=1))


def kernel(devices, tap_scale, streams_hbm, filter_hbm, grad_hbm, *refs):
    tables_hbm = refs[:9]
    mixed_ref, grads_ref, taps_ref = refs[9:12]
    outgoing, arrived, results, returned = refs[12:16]
    tables = refs[16:25]
    streams_ref, filter_ref, grad_ref = refs[25:28]
    input_sem, table_sem, out_send, out_recv, back_send, back_recv, self_sem = refs[28:]
    channels, lanes = filter_ref.shape
    me = lax.axis_index("ctx")
    tp = lax.axis_index("tp")
    barrier = pltpu.get_barrier_semaphore()

    plane = ACROSS * 2
    planes = devices // plane
    zed = me // plane
    side = lax.rem(me, plane) // ACROSS
    why = lax.rem(me, ACROSS)
    whys = [lax.rem(why + turn, ACROSS) for turn in range(ACROSS)]
    sides = [side * ACROSS, (1 - side) * ACROSS]
    far_turns = (2, 1, 3, 0)
    spots = [sides[flip] + whys[turn] for turn in far_turns for flip in (1, 0)]

    parity = lax.rem(tp, 2)
    home = me // 2
    owner = lax.rem(me, 2) == parity
    level = why - lax.rem(why, 2) + parity
    mates = [
        (sides[flip] + lax.rem(level + turn, ACROSS)) // 2 for turn in (2, 0) for flip in (1, 0)
    ]

    def plane_of(step):
        half = planes // 2
        back = (step + 1) // 2
        jump = lax.select(lax.rem(step, 2) == 0, half - back, half + back)
        return lax.rem(zed + jump, planes) * plane

    @pl.when(owner)
    def _():
        def greet(peer):
            pl.semaphore_signal(barrier, inc=1, device_id=(peer, tp), device_id_type=MESH)

        @pl.loop(0, planes - 1)
        def _(step):
            start = plane_of(step)
            for spot in spots:
                greet(start + spot)

        for spot in spots[:-1]:
            greet(zed * plane + spot)

    inputs = [
        pltpu.make_async_copy(source, target, input_sem.at[at])
        for at, (source, target) in enumerate(
            zip((streams_hbm, filter_hbm, grad_hbm), (streams_ref, filter_ref, grad_ref))
        )
    ]
    loads = [
        pltpu.make_async_copy(source, target, table_sem.at[at])
        for at, (source, target) in enumerate(zip(tables_hbm, tables))
    ]
    for load in inputs + loads:
        load.start()
    for load in inputs:
        load.wait()
    query = streams_ref[0].astype(jnp.float32)
    key = streams_ref[1].astype(jnp.float32)
    value = streams_ref[2].astype(jnp.float32)
    upstream = grad_ref[...].astype(jnp.float32)
    outgoing[:, 0, 0:lanes] = key * value
    outgoing[:, 0, lanes : 2 * lanes] = filter_ref[...] * tap_scale
    outgoing[:, 0, 2 * lanes : 3 * lanes] = query * upstream
    for load in loads:
        load.wait()

    @pl.when(owner)
    def _():
        pl.semaphore_wait(barrier, channels - 1)

    @pl.when(jnp.logical_not(owner))
    def _():
        pl.semaphore_wait(barrier, channels)

    def send_out(number):
        pltpu.make_async_remote_copy(
            src_ref=outgoing.at[number],
            dst_ref=arrived.at[me],
            send_sem=out_send,
            recv_sem=out_recv,
            device_id=(number * 2 + parity, tp),
            device_id_type=MESH,
        ).start()

    def send_back(target):
        pltpu.make_async_remote_copy(
            src_ref=results.at[target],
            dst_ref=returned.at[home],
            send_sem=back_send,
            recv_sem=back_recv,
            device_id=(target, tp),
            device_id_type=MESH,
        ).start()

    def block_copy(block, send_sem, recv_sem):
        return pltpu.make_async_remote_copy(
            src_ref=block,
            dst_ref=block,
            send_sem=send_sem,
            recv_sem=recv_sem,
            device_id=(lax.rem(me + 1, devices), tp),
            device_id_type=MESH,
        )

    def keep(source, target):
        copy = pltpu.make_async_copy(source, target, self_sem)
        copy.start()
        copy.wait()

    @pl.loop(0, planes - 1)
    def _(step):
        start = plane_of(step) // 2
        for mate in mates:
            send_out(start + mate)

    for mate in mates[:-1]:
        send_out(zed * (plane // 2) + mate)

    @pl.when(jnp.logical_not(owner))
    def _():
        send_out(home)

    @pl.when(owner)
    def _():
        keep(outgoing.at[home], arrived.at[me])
        block_copy(arrived.at[pl.ds(0, devices - 1)], out_send, out_recv).wait_recv()
        signal = jnp.concatenate(
            [arrived[:, 0, at * lanes : (at + 1) * lanes] for at in range(3)], axis=1
        )
        final = convolve(signal, tables, devices, lanes)
        for at in range(3):
            results[:, 0, at * lanes : (at + 1) * lanes] = final[:, at * lanes : (at + 1) * lanes]

        def back_plane(start):
            for spot in spots:
                send_back(start + spot)

        @pl.loop(0, FIRST)
        def _(step):
            number = lax.rem(zed + step, FIRST)

            @pl.when(number != zed)
            def _():
                back_plane(number * plane)

        @pl.loop(0, planes - 1)
        def _(step):
            start = plane_of(step)

            @pl.when(start >= FIRST * plane)
            def _():
                back_plane(start)

        for spot in spots[:-1]:
            send_back(zed * plane + spot)
        keep(results.at[me], returned.at[home])
        block_copy(returned.at[pl.ds(0, channels - 1)], back_send, back_recv).wait_recv()

    @pl.when(jnp.logical_not(owner))
    def _():
        block_copy(returned, back_send, back_recv).wait_recv()

    long_conv = returned[:, 0, 0:lanes]
    grad_gated = returned[:, 0, lanes : 2 * lanes]
    mixed_ref[...] = (streams_ref[0].astype(jnp.float32) * long_conv).astype(jnp.bfloat16)
    grads_ref[0] = (grad_ref[...].astype(jnp.float32) * long_conv).astype(jnp.bfloat16)
    grads_ref[1] = (grad_gated * streams_ref[2].astype(jnp.float32)).astype(jnp.bfloat16)
    grads_ref[2] = (grad_gated * streams_ref[1].astype(jnp.float32)).astype(jnp.bfloat16)
    taps_ref[...] = returned[:, 0, 2 * lanes : 3 * lanes] * tap_scale

    @pl.when(owner)
    def _():
        block_copy(outgoing.at[pl.ds(0, channels - 1)], out_send, out_recv).wait_send()
        block_copy(results.at[pl.ds(0, devices - 1)], back_send, back_recv).wait_send()

    @pl.when(jnp.logical_not(owner))
    def _():
        block_copy(outgoing, out_send, out_recv).wait_send()


def local(devices, streams, filter_raw, grad_output):
    channels, lanes = filter_raw.shape
    tap_scale = 1.0 / math.sqrt(lanes * devices)
    tables = [jnp.asarray(table) for table in make_tables(devices, lanes)]
    vmem = pl.BlockSpec(memory_space=pltpu.VMEM)
    anywhere = pl.BlockSpec(memory_space=pl.ANY)
    width = 3 * lanes
    inputs = (streams, filter_raw, grad_output)
    operands = [pltpu.with_memory_space_constraint(x, pltpu.HBM) for x in (*inputs, *tables)]
    return pl.pallas_call(
        functools.partial(kernel, devices, tap_scale),
        out_shape=(
            jax.ShapeDtypeStruct((channels, lanes), jnp.bfloat16),
            jax.ShapeDtypeStruct((3, channels, lanes), jnp.bfloat16),
            jax.ShapeDtypeStruct((channels, lanes), jnp.float32),
        ),
        in_specs=[anywhere] * len(operands),
        out_specs=(vmem, vmem, vmem),
        scratch_shapes=[
            pltpu.VMEM((channels, 1, width), jnp.float32),
            pltpu.VMEM((devices, 1, width), jnp.float32),
            pltpu.VMEM((devices, 1, width), jnp.float32),
            pltpu.VMEM((channels, 1, width), jnp.float32),
        ]
        + [pltpu.VMEM(table.shape, table.dtype) for table in tables]
        + [pltpu.VMEM(x.shape, x.dtype) for x in inputs]
        + [pltpu.SemaphoreType.DMA((3,)), pltpu.SemaphoreType.DMA((len(tables),))]
        + [pltpu.SemaphoreType.DMA] * 5,
        compiler_params=pltpu.CompilerParams(
            collective_id=0, has_side_effects=True, vmem_limit_bytes=32 << 20
        ),
    )(*operands)


def solution(mesh):
    devices = mesh.shape["ctx"]
    in_specs = (P(None, "tp", "ctx"), P("tp", "ctx"), P("tp", "ctx"))
    out_specs = (P("tp", "ctx"), P(None, "tp", "ctx"), P("tp", "ctx"))

    def program(streams, filter_raw, grad_output):
        return local(devices, streams, filter_raw, grad_output)

    return jax.shard_map(
        program, mesh=mesh, in_specs=in_specs, out_specs=out_specs, check_vma=False
    )
```

```python
import functools
import math

import jax
import jax.numpy as jnp
import numpy as np
from jax import lax
from jax.experimental import pallas as pl
from jax.experimental.pallas import tpu as pltpu
from jax.sharding import PartitionSpec as P

MESH = pl.DeviceIdType.MESH
ACROSS = 4
FIRST = 4


def split_table(table):
    high = table.astype(jnp.bfloat16)
    low = (table - high.astype(np.float64)).astype(jnp.bfloat16)
    return high, low


def make_tables(rows, lanes):
    length = 2 * rows * lanes
    place = np.arange(rows, dtype=np.int64)
    twice = 2 * np.arange(rows, dtype=np.int64) + 1
    column = np.arange(lanes, dtype=np.int64)
    angle = 2.0 * np.pi / (4 * rows) * (twice[:, None] * place[None, :] % (4 * rows))
    outer = np.concatenate([np.cos(angle), -np.sin(angle)], axis=0)
    angle = 2.0 * np.pi / lanes * (column[:, None] * column[None, :] % lanes)
    cosine, sine = np.cos(angle), np.sin(angle)
    inner = np.block([[cosine, -sine], [sine, cosine]])
    angle = 2.0 * np.pi / (2 * length) * (twice[:, None] * column[None, :] % (2 * length))
    twist = np.stack([np.cos(angle), np.sin(angle)]).astype(np.float32)
    scale = 2.0 / length
    tables = []
    for table in (outer, inner, inner.T, outer.T * scale):
        tables.extend(split_table(table))
    return tables + [twist]


def split_value(value):
    high = value.astype(jnp.bfloat16)
    low = (value - high.astype(jnp.float32)).astype(jnp.bfloat16)
    return high, low


def dot(left, right):
    return jnp.dot(left, right, preferred_element_type=jnp.float32)


def table_times(high, low, value):
    value_high, value_low = split_value(value)
    return dot(high[...], value_high) + (dot(high[...], value_low) + dot(low[...], value_high))


def times_table(value, high, low):
    value_high, value_low = split_value(value)
    return dot(value_high, high[...]) + (dot(value_low, high[...]) + dot(value_high, low[...]))


def convolve(signal, tables, rows_count, lanes):
    outer_high, outer_low, inner_high, inner_low = tables[:4]
    back_high, back_low, final_high, final_low, twist = tables[4:]
    cosine, sine = twist[0], twist[1]
    rows = table_times(outer_high, outer_low, signal)
    spectra = []
    for at in range(3):
        real = rows[:rows_count, at * lanes : (at + 1) * lanes]
        imag = rows[rows_count:, at * lanes : (at + 1) * lanes]
        turned = jnp.concatenate([real * cosine + imag * sine, imag * cosine - real * sine], axis=1)
        both = times_table(turned, inner_high, inner_low)
        spectra.append((both[:, :lanes], both[:, lanes:]))
    (gated_r, gated_i), (taps_r, taps_i), (grad_r, grad_i) = spectra
    products = (
        (gated_r * taps_r - gated_i * taps_i, gated_r * taps_i + gated_i * taps_r),
        (grad_r * taps_r + grad_i * taps_i, grad_i * taps_r - grad_r * taps_i),
        (grad_r * gated_r + grad_i * gated_i, grad_i * gated_r - grad_r * gated_i),
    )
    columns = []
    for real, imag in products:
        both = times_table(jnp.concatenate([real, imag], axis=1), back_high, back_low)
        real, imag = both[:, :lanes], both[:, lanes:]
        columns.append(
            jnp.concatenate([real * cosine - imag * sine, imag * cosine + real * sine], axis=0)
        )
    return table_times(final_high, final_low, jnp.concatenate(columns, axis=1))


def kernel(devices, tap_scale, streams_hbm, filter_hbm, grad_hbm, *refs):
    tables_hbm = refs[:9]
    mixed_ref, grads_ref, taps_ref = refs[9:12]
    outgoing, arrived, results, returned = refs[12:16]
    tables = refs[16:25]
    streams_ref, filter_ref, grad_ref = refs[25:28]
    input_sem, table_sem, out_send, out_recv, back_send, back_recv = refs[28:]
    channels, lanes = filter_ref.shape
    me = lax.axis_index("ctx")
    tp = lax.axis_index("tp")
    barrier = pltpu.get_barrier_semaphore()

    plane = ACROSS * 2
    planes = devices // plane
    zed = me // plane
    side = lax.rem(me, plane) // ACROSS
    why = lax.rem(me, ACROSS)
    whys = [lax.rem(why + turn, ACROSS) for turn in range(ACROSS)]
    sides = [side * ACROSS, (1 - side) * ACROSS]
    far_turns = (2, 1, 3, 0)
    spots = [sides[flip] + whys[turn] for turn in far_turns for flip in (1, 0)]

    parity = lax.rem(tp, 2)
    across_x = 2 * (1 - tp // 2)
    keeper = across_x + 1
    served = across_x + lax.rem(me, 2)
    home = me // 2
    owner = parity == 1
    level = why - lax.rem(why, 2) + parity
    mates = [
        (sides[flip] + lax.rem(level + turn, ACROSS)) // 2 for turn in (2, 0) for flip in (1, 0)
    ]

    def plane_of(step):
        half = planes // 2
        back = (step + 1) // 2
        jump = lax.select(lax.rem(step, 2) == 0, half - back, half + back)
        return lax.rem(zed + jump, planes) * plane

    @pl.when(owner)
    def _():
        def greet(peer):
            pl.semaphore_signal(barrier, inc=1, device_id=(peer, served), device_id_type=MESH)

        @pl.loop(0, planes)
        def _(step):
            start = plane_of(step)
            for spot in spots:
                greet(start + spot)

    inputs = [
        pltpu.make_async_copy(source, target, input_sem.at[at])
        for at, (source, target) in enumerate(
            zip((streams_hbm, filter_hbm, grad_hbm), (streams_ref, filter_ref, grad_ref))
        )
    ]
    loads = [
        pltpu.make_async_copy(source, target, table_sem.at[at])
        for at, (source, target) in enumerate(zip(tables_hbm, tables))
    ]
    for load in inputs + loads:
        load.start()
    for load in inputs:
        load.wait()
    query = streams_ref[0].astype(jnp.float32)
    key = streams_ref[1].astype(jnp.float32)
    value = streams_ref[2].astype(jnp.float32)
    upstream = grad_ref[...].astype(jnp.float32)
    outgoing[:, 0, 0:lanes] = key * value
    outgoing[:, 0, lanes : 2 * lanes] = filter_ref[...] * tap_scale
    outgoing[:, 0, 2 * lanes : 3 * lanes] = query * upstream
    for load in loads:
        load.wait()

    pl.semaphore_wait(barrier, channels)

    def send_out(number):
        pltpu.make_async_remote_copy(
            src_ref=outgoing.at[number],
            dst_ref=arrived.at[me],
            send_sem=out_send,
            recv_sem=out_recv,
            device_id=(number * 2 + parity, keeper),
            device_id_type=MESH,
        ).start()

    def send_back(target):
        pltpu.make_async_remote_copy(
            src_ref=results.at[target],
            dst_ref=returned.at[home],
            send_sem=back_send,
            recv_sem=back_recv,
            device_id=(target, served),
            device_id_type=MESH,
        ).start()

    def block_copy(block, send_sem, recv_sem):
        return pltpu.make_async_remote_copy(
            src_ref=block,
            dst_ref=block,
            send_sem=send_sem,
            recv_sem=recv_sem,
            device_id=(me, across_x),
            device_id_type=MESH,
        )

    @pl.loop(0, planes)
    def _(step):
        start = plane_of(step) // 2
        for mate in mates:
            send_out(start + mate)

    @pl.when(owner)
    def _():
        block_copy(arrived, out_send, out_recv).wait_recv()
        signal = jnp.concatenate(
            [arrived[:, 0, at * lanes : (at + 1) * lanes] for at in range(3)], axis=1
        )
        final = convolve(signal, tables, devices, lanes)
        for at in range(3):
            results[:, 0, at * lanes : (at + 1) * lanes] = final[:, at * lanes : (at + 1) * lanes]

        def back_plane(start):
            for spot in spots:
                send_back(start + spot)

        @pl.loop(0, FIRST)
        def _(step):
            back_plane(lax.rem(zed + step, FIRST) * plane)

        @pl.loop(0, planes)
        def _(step):
            start = plane_of(step)

            @pl.when(start >= FIRST * plane)
            def _():
                back_plane(start)

    block_copy(returned, back_send, back_recv).wait_recv()
    long_conv = returned[:, 0, 0:lanes]
    grad_gated = returned[:, 0, lanes : 2 * lanes]
    mixed_ref[...] = (streams_ref[0].astype(jnp.float32) * long_conv).astype(jnp.bfloat16)
    grads_ref[0] = (grad_ref[...].astype(jnp.float32) * long_conv).astype(jnp.bfloat16)
    grads_ref[1] = (grad_gated * streams_ref[2].astype(jnp.float32)).astype(jnp.bfloat16)
    grads_ref[2] = (grad_gated * streams_ref[1].astype(jnp.float32)).astype(jnp.bfloat16)
    taps_ref[...] = returned[:, 0, 2 * lanes : 3 * lanes] * tap_scale

    block_copy(outgoing, out_send, out_recv).wait_send()

    @pl.when(owner)
    def _():
        block_copy(results, back_send, back_recv).wait_send()


def local(devices, streams, filter_raw, grad_output):
    channels, lanes = filter_raw.shape
    tap_scale = 1.0 / math.sqrt(lanes * devices)
    tables = [jnp.asarray(table) for table in make_tables(devices, lanes)]
    vmem = pl.BlockSpec(memory_space=pltpu.VMEM)
    anywhere = pl.BlockSpec(memory_space=pl.ANY)
    width = 3 * lanes
    inputs = (streams, filter_raw, grad_output)
    operands = [pltpu.with_memory_space_constraint(x, pltpu.HBM) for x in (*inputs, *tables)]
    return pl.pallas_call(
        functools.partial(kernel, devices, tap_scale),
        out_shape=(
            jax.ShapeDtypeStruct((channels, lanes), jnp.bfloat16),
            jax.ShapeDtypeStruct((3, channels, lanes), jnp.bfloat16),
            jax.ShapeDtypeStruct((channels, lanes), jnp.float32),
        ),
        in_specs=[anywhere] * len(operands),
        out_specs=(vmem, vmem, vmem),
        scratch_shapes=[
            pltpu.VMEM((channels, 1, width), jnp.float32),
            pltpu.VMEM((devices, 1, width), jnp.float32),
            pltpu.VMEM((devices, 1, width), jnp.float32),
            pltpu.VMEM((channels, 1, width), jnp.float32),
        ]
        + [pltpu.VMEM(table.shape, table.dtype) for table in tables]
        + [pltpu.VMEM(x.shape, x.dtype) for x in inputs]
        + [pltpu.SemaphoreType.DMA((3,)), pltpu.SemaphoreType.DMA((len(tables),))]
        + [pltpu.SemaphoreType.DMA] * 4,
        compiler_params=pltpu.CompilerParams(
            collective_id=0, has_side_effects=True, vmem_limit_bytes=32 << 20
        ),
    )(*operands)


def solution(mesh):
    devices = mesh.shape["ctx"]
    in_specs = (P(None, "tp", "ctx"), P("tp", "ctx"), P("tp", "ctx"))
    out_specs = (P("tp", "ctx"), P(None, "tp", "ctx"), P("tp", "ctx"))

    def program(streams, filter_raw, grad_output):
        return local(devices, streams, filter_raw, grad_output)

    return jax.shard_map(
        program, mesh=mesh, in_specs=in_specs, out_specs=out_specs, check_vma=False
    )
```

```python
import functools
import math

import jax
import jax.numpy as jnp
import numpy as np
from jax import lax
from jax.experimental import pallas as pl
from jax.experimental.pallas import tpu as pltpu
from jax.sharding import PartitionSpec as P

MESH = pl.DeviceIdType.MESH
ACROSS = 4
FIRST = 4


def split_table(table):
    high = table.astype(jnp.bfloat16)
    low = (table - high.astype(np.float64)).astype(jnp.bfloat16)
    return high, low


def make_tables(rows, lanes):
    length = 2 * rows * lanes
    place = np.arange(rows, dtype=np.int64)
    twice = 2 * np.arange(rows, dtype=np.int64) + 1
    column = np.arange(lanes, dtype=np.int64)
    angle = 2.0 * np.pi / (4 * rows) * (twice[:, None] * place[None, :] % (4 * rows))
    outer = np.concatenate([np.cos(angle), -np.sin(angle)], axis=0)
    angle = 2.0 * np.pi / lanes * (column[:, None] * column[None, :] % lanes)
    cosine, sine = np.cos(angle), np.sin(angle)
    inner = np.block([[cosine, -sine], [sine, cosine]])
    angle = 2.0 * np.pi / (2 * length) * (twice[:, None] * column[None, :] % (2 * length))
    twist = np.stack([np.cos(angle), np.sin(angle)]).astype(np.float32)
    scale = 2.0 / length
    tables = []
    for table in (outer, inner, inner.T, outer.T * scale):
        tables.extend(split_table(table))
    return tables + [twist]


def split_value(value):
    high = value.astype(jnp.bfloat16)
    low = (value - high.astype(jnp.float32)).astype(jnp.bfloat16)
    return high, low


def dot(left, right):
    return jnp.dot(left, right, preferred_element_type=jnp.float32)


def table_times(high, low, value):
    value_high, value_low = split_value(value)
    return dot(high[...], value_high) + (dot(high[...], value_low) + dot(low[...], value_high))


def times_table(value, high, low):
    value_high, value_low = split_value(value)
    return dot(value_high, high[...]) + (dot(value_low, high[...]) + dot(value_high, low[...]))


def convolve(signal, tables, rows_count, lanes):
    outer_high, outer_low, inner_high, inner_low = tables[:4]
    back_high, back_low, final_high, final_low, twist = tables[4:]
    cosine, sine = twist[0], twist[1]
    rows = table_times(outer_high, outer_low, signal)
    spectra = []
    for at in range(3):
        real = rows[:rows_count, at * lanes : (at + 1) * lanes]
        imag = rows[rows_count:, at * lanes : (at + 1) * lanes]
        turned = jnp.concatenate([real * cosine + imag * sine, imag * cosine - real * sine], axis=1)
        both = times_table(turned, inner_high, inner_low)
        spectra.append((both[:, :lanes], both[:, lanes:]))
    (gated_r, gated_i), (taps_r, taps_i), (grad_r, grad_i) = spectra
    products = (
        (gated_r * taps_r - gated_i * taps_i, gated_r * taps_i + gated_i * taps_r),
        (grad_r * taps_r + grad_i * taps_i, grad_i * taps_r - grad_r * taps_i),
        (grad_r * gated_r + grad_i * gated_i, grad_i * gated_r - grad_r * gated_i),
    )
    columns = []
    for real, imag in products:
        both = times_table(jnp.concatenate([real, imag], axis=1), back_high, back_low)
        real, imag = both[:, :lanes], both[:, lanes:]
        columns.append(
            jnp.concatenate([real * cosine - imag * sine, imag * cosine + real * sine], axis=0)
        )
    return table_times(final_high, final_low, jnp.concatenate(columns, axis=1))


def kernel(devices, tap_scale, streams_hbm, filter_hbm, grad_hbm, *refs):
    tables_hbm = refs[:9]
    mixed_ref, grads_ref, taps_ref = refs[9:12]
    outgoing, arrived, results, returned = refs[12:16]
    tables = refs[16:25]
    streams_ref, filter_ref, grad_ref = refs[25:28]
    input_sem, table_sem, out_send, out_recv, back_send, back_recv = refs[28:]
    channels, lanes = filter_ref.shape
    me = lax.axis_index("ctx")
    tp = lax.axis_index("tp")
    barrier = pltpu.get_barrier_semaphore()

    plane = ACROSS * 2
    planes = devices // plane
    zed = me // plane
    side = lax.rem(me, plane) // ACROSS
    why = lax.rem(me, ACROSS)
    whys = [lax.rem(why + turn, ACROSS) for turn in range(ACROSS)]
    sides = [side * ACROSS, (1 - side) * ACROSS]
    far_turns = (2, 1, 3, 0)
    spots = [sides[flip] + whys[turn] for turn in far_turns for flip in (1, 0)]

    parity = lax.rem(tp, 2)
    across_x = 2 * (1 - tp // 2)
    keeper = across_x + 1
    served = across_x + lax.rem(me, 2)
    home = me // 2
    owner = parity == 1
    level = why - lax.rem(why, 2) + parity
    mates = [
        (sides[flip] + lax.rem(level + turn, ACROSS)) // 2 for turn in (2, 0) for flip in (1, 0)
    ]

    def plane_of(step):
        half = planes // 2
        back = (step + 1) // 2
        jump = lax.select(lax.rem(step, 2) == 0, half - back, half + back)
        return lax.rem(zed + jump, planes) * plane

    @pl.when(owner)
    def _():
        def greet(peer):
            pl.semaphore_signal(barrier, inc=1, device_id=(peer, served), device_id_type=MESH)

        @pl.loop(0, planes)
        def _(step):
            start = plane_of(step)
            for spot in spots:
                greet(start + spot)

    inputs = [
        pltpu.make_async_copy(source, target, input_sem.at[at])
        for at, (source, target) in enumerate(
            zip((streams_hbm, filter_hbm, grad_hbm), (streams_ref, filter_ref, grad_ref))
        )
    ]
    loads = [
        pltpu.make_async_copy(source, target, table_sem.at[at])
        for at, (source, target) in enumerate(zip(tables_hbm, tables))
    ]
    for load in inputs + loads:
        load.start()
    for load in inputs:
        load.wait()
    query = streams_ref[0].astype(jnp.float32)
    key = streams_ref[1].astype(jnp.float32)
    value = streams_ref[2].astype(jnp.float32)
    upstream = grad_ref[...].astype(jnp.float32)
    outgoing[:, 0, 0:lanes] = key * value
    outgoing[:, 0, lanes : 2 * lanes] = filter_ref[...] * tap_scale
    outgoing[:, 0, 2 * lanes : 3 * lanes] = query * upstream
    for load in loads:
        load.wait()

    pl.semaphore_wait(barrier, channels)

    def send_out(number):
        pltpu.make_async_remote_copy(
            src_ref=outgoing.at[number],
            dst_ref=arrived.at[me],
            send_sem=out_send,
            recv_sem=out_recv,
            device_id=(number * 2 + parity, keeper),
            device_id_type=MESH,
        ).start()

    def send_back(target):
        pltpu.make_async_remote_copy(
            src_ref=results.at[target],
            dst_ref=returned.at[home],
            send_sem=back_send,
            recv_sem=back_recv,
            device_id=(target, served),
            device_id_type=MESH,
        ).start()

    def block_copy(block, send_sem, recv_sem):
        return pltpu.make_async_remote_copy(
            src_ref=block,
            dst_ref=block,
            send_sem=send_sem,
            recv_sem=recv_sem,
            device_id=(me, across_x),
            device_id_type=MESH,
        )

    @pl.loop(0, planes)
    def _(step):
        start = plane_of(step) // 2
        for mate in mates:
            send_out(start + mate)

    @pl.when(owner)
    def _():
        block_copy(arrived, out_send, out_recv).wait_recv()
        signal = jnp.concatenate(
            [arrived[:, 0, at * lanes : (at + 1) * lanes] for at in range(3)], axis=1
        )
        final = convolve(signal, tables, devices, lanes)
        for at in range(3):
            results[:, 0, at * lanes : (at + 1) * lanes] = final[:, at * lanes : (at + 1) * lanes]

        def back_plane(start):
            for spot in spots:
                send_back(start + spot)

        @pl.loop(0, FIRST)
        def _(step):
            back_plane(lax.rem(zed + step, FIRST) * plane)

        @pl.loop(0, planes)
        def _(step):
            start = plane_of(step)

            @pl.when(start >= FIRST * plane)
            def _():
                back_plane(start)

    block_copy(returned, back_send, back_recv).wait_recv()
    long_conv = returned[:, 0, 0:lanes]
    grad_gated = returned[:, 0, lanes : 2 * lanes]
    mixed_ref[...] = (streams_ref[0].astype(jnp.float32) * long_conv).astype(jnp.bfloat16)
    grads_ref[0] = (grad_ref[...].astype(jnp.float32) * long_conv).astype(jnp.bfloat16)
    grads_ref[1] = (grad_gated * streams_ref[2].astype(jnp.float32)).astype(jnp.bfloat16)
    grads_ref[2] = (grad_gated * streams_ref[1].astype(jnp.float32)).astype(jnp.bfloat16)
    taps_ref[...] = returned[:, 0, 2 * lanes : 3 * lanes] * tap_scale

    block_copy(outgoing, out_send, out_recv).wait_send()

    @pl.when(owner)
    def _():
        block_copy(results, back_send, back_recv).wait_send()


def store_kernel(*refs):
    copies = [
        pltpu.make_async_copy(source, target, refs[-1].at[at])
        for at, (source, target) in enumerate(zip(refs[:3], refs[3:6]))
    ]
    for copy in copies:
        copy.start()
    for copy in copies:
        copy.wait()


def local(devices, streams, filter_raw, grad_output):
    channels, lanes = filter_raw.shape
    tap_scale = 1.0 / math.sqrt(lanes * devices)
    tables = [jnp.asarray(table) for table in make_tables(devices, lanes)]
    vmem = pl.BlockSpec(memory_space=pltpu.VMEM)
    anywhere = pl.BlockSpec(memory_space=pl.ANY)
    width = 3 * lanes
    inputs = (streams, filter_raw, grad_output)
    operands = [pltpu.with_memory_space_constraint(x, pltpu.HBM) for x in (*inputs, *tables)]
    results = pl.pallas_call(
        functools.partial(kernel, devices, tap_scale),
        out_shape=(
            jax.ShapeDtypeStruct((channels, lanes), jnp.bfloat16),
            jax.ShapeDtypeStruct((3, channels, lanes), jnp.bfloat16),
            jax.ShapeDtypeStruct((channels, lanes), jnp.float32),
        ),
        in_specs=[anywhere] * len(operands),
        out_specs=(vmem, vmem, vmem),
        scratch_shapes=[
            pltpu.VMEM((channels, 1, width), jnp.float32),
            pltpu.VMEM((devices, 1, width), jnp.float32),
            pltpu.VMEM((devices, 1, width), jnp.float32),
            pltpu.VMEM((channels, 1, width), jnp.float32),
        ]
        + [pltpu.VMEM(table.shape, table.dtype) for table in tables]
        + [pltpu.VMEM(x.shape, x.dtype) for x in inputs]
        + [pltpu.SemaphoreType.DMA((3,)), pltpu.SemaphoreType.DMA((len(tables),))]
        + [pltpu.SemaphoreType.DMA] * 4,
        compiler_params=pltpu.CompilerParams(
            collective_id=0, has_side_effects=True, vmem_limit_bytes=32 << 20
        ),
    )(*operands)
    results = [pltpu.with_memory_space_constraint(x, pltpu.VMEM) for x in results]
    shapes = tuple(jax.ShapeDtypeStruct(x.shape, x.dtype) for x in results)
    return pl.pallas_call(
        store_kernel,
        out_shape=shapes,
        in_specs=[anywhere] * 3,
        out_specs=[anywhere] * 3,
        scratch_shapes=[pltpu.SemaphoreType.DMA((3,))],
        compiler_params=pltpu.CompilerParams(vmem_limit_bytes=8 << 20),
    )(*results)


def solution(mesh):
    devices = mesh.shape["ctx"]
    in_specs = (P(None, "tp", "ctx"), P("tp", "ctx"), P("tp", "ctx"))
    out_specs = (P("tp", "ctx"), P(None, "tp", "ctx"), P("tp", "ctx"))

    def program(streams, filter_raw, grad_output):
        return local(devices, streams, filter_raw, grad_output)

    return jax.shard_map(
        program, mesh=mesh, in_specs=in_specs, out_specs=out_specs, check_vma=False
    )
```

```python
import functools
import math

import jax
import jax.numpy as jnp
import numpy as np
from jax import lax
from jax.experimental import pallas as pl
from jax.experimental.pallas import tpu as pltpu
from jax.sharding import PartitionSpec as P

MESH = pl.DeviceIdType.MESH
ACROSS = 4
FIRST = 4


def split_table(table):
    high = table.astype(jnp.bfloat16)
    low = (table - high.astype(np.float64)).astype(jnp.bfloat16)
    return high, low


def make_tables(rows, lanes):
    length = 2 * rows * lanes
    place = np.arange(rows, dtype=np.int64)
    twice = 2 * np.arange(rows, dtype=np.int64) + 1
    column = np.arange(lanes, dtype=np.int64)
    angle = 2.0 * np.pi / (4 * rows) * (twice[:, None] * place[None, :] % (4 * rows))
    outer = np.concatenate([np.cos(angle), -np.sin(angle)], axis=0)
    angle = 2.0 * np.pi / lanes * (column[:, None] * column[None, :] % lanes)
    cosine, sine = np.cos(angle), np.sin(angle)
    inner = np.block([[cosine, -sine], [sine, cosine]])
    angle = 2.0 * np.pi / (2 * length) * (twice[:, None] * column[None, :] % (2 * length))
    twist = np.stack([np.cos(angle), np.sin(angle)]).astype(np.float32)
    scale = 2.0 / length
    tables = []
    for table in (outer, inner, inner.T, outer.T * scale):
        tables.extend(split_table(table))
    return tables + [twist]


def split_value(value):
    high = value.astype(jnp.bfloat16)
    low = (value - high.astype(jnp.float32)).astype(jnp.bfloat16)
    return high, low


def dot(left, right):
    return jnp.dot(left, right, preferred_element_type=jnp.float32)


def table_times(high, low, value):
    value_high, value_low = split_value(value)
    return dot(high[...], value_high) + (dot(high[...], value_low) + dot(low[...], value_high))


def times_table(value, high, low):
    value_high, value_low = split_value(value)
    return dot(value_high, high[...]) + (dot(value_low, high[...]) + dot(value_high, low[...]))


def convolve(signal, tables, rows_count, lanes):
    outer_high, outer_low, inner_high, inner_low = tables[:4]
    back_high, back_low, final_high, final_low, twist = tables[4:]
    cosine, sine = twist[0], twist[1]
    rows = table_times(outer_high, outer_low, signal)
    spectra = []
    for at in range(3):
        real = rows[:rows_count, at * lanes : (at + 1) * lanes]
        imag = rows[rows_count:, at * lanes : (at + 1) * lanes]
        turned = jnp.concatenate([real * cosine + imag * sine, imag * cosine - real * sine], axis=1)
        both = times_table(turned, inner_high, inner_low)
        spectra.append((both[:, :lanes], both[:, lanes:]))
    (gated_r, gated_i), (taps_r, taps_i), (grad_r, grad_i) = spectra
    products = (
        (gated_r * taps_r - gated_i * taps_i, gated_r * taps_i + gated_i * taps_r),
        (grad_r * taps_r + grad_i * taps_i, grad_i * taps_r - grad_r * taps_i),
        (grad_r * gated_r + grad_i * gated_i, grad_i * gated_r - grad_r * gated_i),
    )
    columns = []
    for real, imag in products:
        both = times_table(jnp.concatenate([real, imag], axis=1), back_high, back_low)
        real, imag = both[:, :lanes], both[:, lanes:]
        columns.append(
            jnp.concatenate([real * cosine - imag * sine, imag * cosine + real * sine], axis=0)
        )
    return table_times(final_high, final_low, jnp.concatenate(columns, axis=1))


def kernel(devices, tap_scale, streams_hbm, filter_hbm, grad_hbm, *refs):
    tables_hbm = refs[:9]
    mixed_ref, grads_ref, taps_ref = refs[9:12]
    outgoing, arrived, results, returned = refs[12:16]
    tables = refs[16:25]
    streams_ref, filter_ref, grad_ref = refs[25:28]
    input_sem, table_sem, out_send, out_recv, back_send, back_recv, self_sem = refs[28:]
    channels, lanes = filter_ref.shape
    me = lax.axis_index("ctx")
    tp = lax.axis_index("tp")
    barrier = pltpu.get_barrier_semaphore()

    plane = ACROSS * 2
    planes = devices // plane
    zed = me // plane
    side = lax.rem(me, plane) // ACROSS
    why = lax.rem(me, ACROSS)
    whys = [lax.rem(why + turn, ACROSS) for turn in range(ACROSS)]
    sides = [side * ACROSS, (1 - side) * ACROSS]
    far_turns = (2, 1, 3, 0)
    spots = [sides[flip] + whys[turn] for turn in far_turns for flip in (1, 0)]

    core = lax.rem(tp, 2)
    low = tp // 2
    keeper = lax.select(core == 0, 3 - 2 * low, tp)
    served = lax.select(side == low, tp, 2 - 2 * low)
    home = zed * ACROSS + why
    owner = core == 1
    alone = jnp.logical_and(owner, side == low)
    paired = jnp.logical_not(alone)
    mates = [whys[turn] for turn in far_turns]

    def plane_of(step):
        half = planes // 2
        back = (step + 1) // 2
        jump = lax.select(lax.rem(step, 2) == 0, half - back, half + back)
        return lax.rem(zed + jump, planes) * plane

    @pl.when(owner)
    def _():
        def greet(peer):
            pl.semaphore_signal(barrier, inc=1, device_id=(peer, served), device_id_type=MESH)

        @pl.loop(0, planes - 1)
        def _(step):
            start = plane_of(step)
            for spot in spots:
                greet(start + spot)

        for spot in spots[:-1]:
            greet(zed * plane + spot)

        @pl.when(paired)
        def _():
            greet(me)

    inputs = [
        pltpu.make_async_copy(source, target, input_sem.at[at])
        for at, (source, target) in enumerate(
            zip((streams_hbm, filter_hbm, grad_hbm), (streams_ref, filter_ref, grad_ref))
        )
    ]
    loads = [
        pltpu.make_async_copy(source, target, table_sem.at[at])
        for at, (source, target) in enumerate(zip(tables_hbm, tables))
    ]
    for load in inputs + loads:
        load.start()
    for load in inputs:
        load.wait()
    query = streams_ref[0].astype(jnp.float32)
    key = streams_ref[1].astype(jnp.float32)
    value = streams_ref[2].astype(jnp.float32)
    upstream = grad_ref[...].astype(jnp.float32)
    outgoing[0] = key * value
    outgoing[1] = filter_ref[...] * tap_scale
    outgoing[2] = query * upstream
    for load in loads:
        load.wait()

    @pl.when(alone)
    def _():
        pl.semaphore_wait(barrier, channels - 1)

    @pl.when(paired)
    def _():
        pl.semaphore_wait(barrier, channels)

    def send_out(number):
        pltpu.make_async_remote_copy(
            src_ref=outgoing.at[:, pl.ds(number, 1), :],
            dst_ref=arrived.at[:, pl.ds(me, 1), :],
            send_sem=out_send,
            recv_sem=out_recv,
            device_id=(number // ACROSS * plane + low * ACROSS + lax.rem(number, ACROSS), keeper),
            device_id_type=MESH,
        ).start()

    def send_back(target):
        pltpu.make_async_remote_copy(
            src_ref=results.at[:, pl.ds(target, 1), :],
            dst_ref=returned.at[:, pl.ds(home, 1), :],
            send_sem=back_send,
            recv_sem=back_recv,
            device_id=(target, served),
            device_id_type=MESH,
        ).start()

    def block_copy(block, send_sem, recv_sem):
        return pltpu.make_async_remote_copy(
            src_ref=block,
            dst_ref=block,
            send_sem=send_sem,
            recv_sem=recv_sem,
            device_id=(me, lax.rem(tp + 1, 4)),
            device_id_type=MESH,
        )

    def keep(source, target):
        copy = pltpu.make_async_copy(source, target, self_sem)
        copy.start()
        copy.wait()

    mine = pl.ds(me, 1)
    housed = pl.ds(home, 1)
    most = pl.ds(0, devices - 1)
    many = pl.ds(0, channels - 1)

    @pl.loop(0, planes - 1)
    def _(step):
        start = plane_of(step) // 2
        for mate in mates:
            send_out(start + mate)

    for mate in mates[:-1]:
        send_out(zed * ACROSS + mate)

    @pl.when(paired)
    def _():
        send_out(home)

    @pl.when(owner)
    def _():
        @pl.when(alone)
        def _():
            keep(outgoing.at[:, housed, :], arrived.at[:, mine, :])
            block_copy(arrived.at[:, most, :], out_send, out_recv).wait_recv()

        @pl.when(paired)
        def _():
            block_copy(arrived, out_send, out_recv).wait_recv()

        signal = jnp.concatenate(
            [arrived[at] for at in range(3)], axis=1
        )
        final = convolve(signal, tables, devices, lanes)
        for at in range(3):
            results[at] = final[:, at * lanes : (at + 1) * lanes]

        def back_plane(start):
            for spot in spots:
                send_back(start + spot)

        @pl.loop(0, FIRST)
        def _(step):
            turn = lax.select(jnp.logical_and(alone, low == 1), 0, zed)
            number = lax.rem(turn + step, FIRST)

            @pl.when(number != zed)
            def _():
                back_plane(number * plane)

        @pl.loop(0, planes - 1)
        def _(step):
            start = plane_of(step)

            @pl.when(start >= FIRST * plane)
            def _():
                back_plane(start)

        for spot in spots[:-1]:
            send_back(zed * plane + spot)

        @pl.when(paired)
        def _():
            send_back(me)

    @pl.when(alone)
    def _():
        keep(results.at[:, mine, :], returned.at[:, housed, :])
        block_copy(returned.at[:, many, :], back_send, back_recv).wait_recv()

    @pl.when(paired)
    def _():
        block_copy(returned, back_send, back_recv).wait_recv()

    long_conv = returned[0]
    grad_gated = returned[1]
    mixed_ref[...] = (streams_ref[0].astype(jnp.float32) * long_conv).astype(jnp.bfloat16)
    grads_ref[0] = (grad_ref[...].astype(jnp.float32) * long_conv).astype(jnp.bfloat16)
    grads_ref[1] = (grad_gated * streams_ref[2].astype(jnp.float32)).astype(jnp.bfloat16)
    grads_ref[2] = (grad_gated * streams_ref[1].astype(jnp.float32)).astype(jnp.bfloat16)
    taps_ref[...] = returned[2] * tap_scale

    @pl.when(alone)
    def _():
        block_copy(outgoing.at[:, many, :], out_send, out_recv).wait_send()
        block_copy(results.at[:, most, :], back_send, back_recv).wait_send()

    @pl.when(paired)
    def _():
        block_copy(outgoing, out_send, out_recv).wait_send()

    @pl.when(jnp.logical_and(owner, paired))
    def _():
        block_copy(results, back_send, back_recv).wait_send()


def store_kernel(*refs):
    copies = [
        pltpu.make_async_copy(source, target, refs[-1].at[at])
        for at, (source, target) in enumerate(zip(refs[:3], refs[3:6]))
    ]
    for copy in copies:
        copy.start()
    for copy in copies:
        copy.wait()


def local(devices, streams, filter_raw, grad_output):
    channels, lanes = filter_raw.shape
    tap_scale = 1.0 / math.sqrt(lanes * devices)
    tables = [jnp.asarray(table) for table in make_tables(devices, lanes)]
    vmem = pl.BlockSpec(memory_space=pltpu.VMEM)
    anywhere = pl.BlockSpec(memory_space=pl.ANY)
    inputs = (streams, filter_raw, grad_output)
    operands = [pltpu.with_memory_space_constraint(x, pltpu.HBM) for x in (*inputs, *tables)]
    results = pl.pallas_call(
        functools.partial(kernel, devices, tap_scale),
        out_shape=(
            jax.ShapeDtypeStruct((channels, lanes), jnp.bfloat16),
            jax.ShapeDtypeStruct((3, channels, lanes), jnp.bfloat16),
            jax.ShapeDtypeStruct((channels, lanes), jnp.float32),
        ),
        in_specs=[anywhere] * len(operands),
        out_specs=(vmem, vmem, vmem),
        scratch_shapes=[
            pltpu.VMEM((3, channels, lanes), jnp.float32),
            pltpu.VMEM((3, devices, lanes), jnp.float32),
            pltpu.VMEM((3, devices, lanes), jnp.float32),
            pltpu.VMEM((3, channels, lanes), jnp.float32),
        ]
        + [pltpu.VMEM(table.shape, table.dtype) for table in tables]
        + [pltpu.VMEM(x.shape, x.dtype) for x in inputs]
        + [pltpu.SemaphoreType.DMA((3,)), pltpu.SemaphoreType.DMA((len(tables),))]
        + [pltpu.SemaphoreType.DMA] * 5,
        compiler_params=pltpu.CompilerParams(
            collective_id=0, has_side_effects=True, vmem_limit_bytes=32 << 20
        ),
    )(*operands)
    results = [pltpu.with_memory_space_constraint(x, pltpu.VMEM) for x in results]
    shapes = tuple(jax.ShapeDtypeStruct(x.shape, x.dtype) for x in results)
    return pl.pallas_call(
        store_kernel,
        out_shape=shapes,
        in_specs=[anywhere] * 3,
        out_specs=[anywhere] * 3,
        scratch_shapes=[pltpu.SemaphoreType.DMA((3,))],
        compiler_params=pltpu.CompilerParams(vmem_limit_bytes=8 << 20),
    )(*results)


def solution(mesh):
    devices = mesh.shape["ctx"]
    in_specs = (P(None, "tp", "ctx"), P("tp", "ctx"), P("tp", "ctx"))
    out_specs = (P("tp", "ctx"), P(None, "tp", "ctx"), P("tp", "ctx"))

    def program(streams, filter_raw, grad_output):
        return local(devices, streams, filter_raw, grad_output)

    return jax.shard_map(
        program, mesh=mesh, in_specs=in_specs, out_specs=out_specs, check_vma=False
    )
```

```python
import functools
import math

import jax
import jax.numpy as jnp
import numpy as np
from jax import lax
from jax.experimental import pallas as pl
from jax.experimental.pallas import tpu as pltpu
from jax.sharding import PartitionSpec as P

MESH = pl.DeviceIdType.MESH
ACROSS = 4
FIRST = 4


def split_table(table):
    high = table.astype(jnp.bfloat16)
    low = (table - high.astype(np.float64)).astype(jnp.bfloat16)
    return high, low


def make_tables(rows, lanes):
    length = 2 * rows * lanes
    place = np.arange(rows, dtype=np.int64)
    twice = 2 * np.arange(rows, dtype=np.int64) + 1
    column = np.arange(lanes, dtype=np.int64)
    angle = 2.0 * np.pi / (4 * rows) * (twice[:, None] * place[None, :] % (4 * rows))
    outer = np.concatenate([np.cos(angle), -np.sin(angle)], axis=0)
    angle = 2.0 * np.pi / lanes * (column[:, None] * column[None, :] % lanes)
    cosine, sine = np.cos(angle), np.sin(angle)
    inner = np.block([[cosine, -sine], [sine, cosine]])
    angle = 2.0 * np.pi / (2 * length) * (twice[:, None] * column[None, :] % (2 * length))
    twist = np.stack([np.cos(angle), np.sin(angle)]).astype(np.float32)
    scale = 2.0 / length
    tables = []
    for table in (outer, inner, inner.T, outer.T * scale):
        tables.extend(split_table(table))
    return tables + [twist]


def split_value(value):
    high = value.astype(jnp.bfloat16)
    low = (value - high.astype(jnp.float32)).astype(jnp.bfloat16)
    return high, low


def dot(left, right):
    return jnp.dot(left, right, preferred_element_type=jnp.float32)


def table_times(high, low, value):
    value_high, value_low = split_value(value)
    return dot(high[...], value_high) + (dot(high[...], value_low) + dot(low[...], value_high))


def times_table(value, high, low):
    value_high, value_low = split_value(value)
    return dot(value_high, high[...]) + (dot(value_low, high[...]) + dot(value_high, low[...]))


def convolve(signal, tables, rows_count, lanes):
    outer_high, outer_low, inner_high, inner_low = tables[:4]
    back_high, back_low, final_high, final_low, twist = tables[4:]
    cosine, sine = twist[0], twist[1]
    rows = table_times(outer_high, outer_low, signal)
    spectra = []
    for at in range(3):
        real = rows[:rows_count, at * lanes : (at + 1) * lanes]
        imag = rows[rows_count:, at * lanes : (at + 1) * lanes]
        turned = jnp.concatenate([real * cosine + imag * sine, imag * cosine - real * sine], axis=1)
        both = times_table(turned, inner_high, inner_low)
        spectra.append((both[:, :lanes], both[:, lanes:]))
    (gated_r, gated_i), (taps_r, taps_i), (grad_r, grad_i) = spectra
    products = (
        (gated_r * taps_r - gated_i * taps_i, gated_r * taps_i + gated_i * taps_r),
        (grad_r * taps_r + grad_i * taps_i, grad_i * taps_r - grad_r * taps_i),
        (grad_r * gated_r + grad_i * gated_i, grad_i * gated_r - grad_r * gated_i),
    )
    columns = []
    for real, imag in products:
        both = times_table(jnp.concatenate([real, imag], axis=1), back_high, back_low)
        real, imag = both[:, :lanes], both[:, lanes:]
        columns.append(
            jnp.concatenate([real * cosine - imag * sine, imag * cosine + real * sine], axis=0)
        )
    return table_times(final_high, final_low, jnp.concatenate(columns, axis=1))


def kernel(devices, tap_scale, streams_hbm, filter_hbm, grad_hbm, *refs):
    tables_hbm = refs[:9]
    mixed_ref, grads_ref, taps_ref = refs[9:12]
    outgoing, arrived, results, returned = refs[12:16]
    tables = refs[16:25]
    streams_ref, filter_ref, grad_ref = refs[25:28]
    input_sem, table_sem, out_send, out_recv, back_send, back_recv, self_sem = refs[28:]
    channels, lanes = filter_ref.shape
    me = lax.axis_index("ctx")
    tp = lax.axis_index("tp")
    barrier = pltpu.get_barrier_semaphore()

    plane = ACROSS * 2
    planes = devices // plane
    zed = me // plane
    side = lax.rem(me, plane) // ACROSS
    why = lax.rem(me, ACROSS)
    whys = [lax.rem(why + turn, ACROSS) for turn in range(ACROSS)]
    sides = [side * ACROSS, (1 - side) * ACROSS]
    far_turns = (2, 1, 3, 0)
    spots = [sides[flip] + whys[turn] for turn in far_turns for flip in (1, 0)]

    core = lax.rem(tp, 2)
    low = tp // 2
    keeper = lax.select(core == 0, 3 - 2 * low, tp)
    served = lax.select(side == low, tp, 2 - 2 * low)
    home = zed * ACROSS + why
    owner = core == 1
    alone = jnp.logical_and(owner, side == low)
    paired = jnp.logical_not(alone)
    mates = [whys[turn] for turn in far_turns]

    def plane_of(step):
        half = planes // 2
        back = (step + 1) // 2
        jump = lax.select(lax.rem(step, 2) == 0, half - back, half + back)
        return lax.rem(zed + jump, planes) * plane

    @pl.when(owner)
    def _():
        def greet(peer):
            pl.semaphore_signal(barrier, inc=1, device_id=(peer, served), device_id_type=MESH)

        @pl.loop(0, planes - 1)
        def _(step):
            start = plane_of(step)
            for spot in spots:
                greet(start + spot)

        for spot in spots[:-1]:
            greet(zed * plane + spot)

        @pl.when(paired)
        def _():
            greet(me)

    inputs = [
        pltpu.make_async_copy(source, target, input_sem.at[at])
        for at, (source, target) in enumerate(
            zip((streams_hbm, filter_hbm, grad_hbm), (streams_ref, filter_ref, grad_ref))
        )
    ]
    loads = [
        pltpu.make_async_copy(source, target, table_sem.at[at])
        for at, (source, target) in enumerate(zip(tables_hbm, tables))
    ]
    for load in inputs + loads:
        load.start()
    for load in inputs:
        load.wait()
    query = streams_ref[0].astype(jnp.float32)
    key = streams_ref[1].astype(jnp.float32)
    value = streams_ref[2].astype(jnp.float32)
    upstream = grad_ref[...].astype(jnp.float32)
    outgoing[0] = key * value
    outgoing[1] = filter_ref[...] * tap_scale
    outgoing[2] = query * upstream
    for load in loads:
        load.wait()

    @pl.when(alone)
    def _():
        pl.semaphore_wait(barrier, channels - 1)

    @pl.when(paired)
    def _():
        pl.semaphore_wait(barrier, channels)

    def send_out(number):
        pltpu.make_async_remote_copy(
            src_ref=outgoing.at[:, pl.ds(number, 1), :],
            dst_ref=arrived.at[:, pl.ds(me, 1), :],
            send_sem=out_send,
            recv_sem=out_recv,
            device_id=(number // ACROSS * plane + low * ACROSS + lax.rem(number, ACROSS), keeper),
            device_id_type=MESH,
        ).start()

    def send_back(target):
        pltpu.make_async_remote_copy(
            src_ref=results.at[:, pl.ds(target, 1), :],
            dst_ref=returned.at[:, pl.ds(home, 1), :],
            send_sem=back_send,
            recv_sem=back_recv,
            device_id=(target, served),
            device_id_type=MESH,
        ).start()

    def block_copy(block, send_sem, recv_sem):
        return pltpu.make_async_remote_copy(
            src_ref=block,
            dst_ref=block,
            send_sem=send_sem,
            recv_sem=recv_sem,
            device_id=(me, lax.rem(tp + 1, 4)),
            device_id_type=MESH,
        )

    def keep(source, target):
        copy = pltpu.make_async_copy(source, target, self_sem)
        copy.start()
        copy.wait()

    mine = pl.ds(me, 1)
    housed = pl.ds(home, 1)
    most = pl.ds(0, devices - 1)
    many = pl.ds(0, channels - 1)

    @pl.loop(0, planes - 1)
    def _(step):
        start = plane_of(step) // 2
        for mate in mates:
            send_out(start + mate)

    for mate in mates[:-1]:
        send_out(zed * ACROSS + mate)

    @pl.when(paired)
    def _():
        send_out(home)

    @pl.when(owner)
    def _():
        @pl.when(alone)
        def _():
            keep(outgoing.at[:, housed, :], arrived.at[:, mine, :])
            block_copy(arrived.at[:, most, :], out_send, out_recv).wait_recv()

        @pl.when(paired)
        def _():
            block_copy(arrived, out_send, out_recv).wait_recv()

        signal = jnp.concatenate(
            [arrived[at] for at in range(3)], axis=1
        )
        final = convolve(signal, tables, devices, lanes)
        for at in range(3):
            results[at] = final[:, at * lanes : (at + 1) * lanes]

        def back_plane(start):
            for spot in spots:
                send_back(start + spot)

        @pl.loop(0, FIRST)
        def _(step):
            turn = lax.select(low == 1, 0, zed)
            number = lax.rem(turn + step, FIRST)

            @pl.when(number != zed)
            def _():
                back_plane(number * plane)

        @pl.loop(0, planes - 1)
        def _(step):
            start = plane_of(step)

            @pl.when(start >= FIRST * plane)
            def _():
                back_plane(start)

        for spot in spots[:-1]:
            send_back(zed * plane + spot)

        @pl.when(paired)
        def _():
            send_back(me)

    @pl.when(alone)
    def _():
        keep(results.at[:, mine, :], returned.at[:, housed, :])
        block_copy(returned.at[:, many, :], back_send, back_recv).wait_recv()

    @pl.when(paired)
    def _():
        block_copy(returned, back_send, back_recv).wait_recv()

    long_conv = returned[0]
    grad_gated = returned[1]
    mixed_ref[...] = (streams_ref[0].astype(jnp.float32) * long_conv).astype(jnp.bfloat16)
    grads_ref[0] = (grad_ref[...].astype(jnp.float32) * long_conv).astype(jnp.bfloat16)
    grads_ref[1] = (grad_gated * streams_ref[2].astype(jnp.float32)).astype(jnp.bfloat16)
    grads_ref[2] = (grad_gated * streams_ref[1].astype(jnp.float32)).astype(jnp.bfloat16)
    taps_ref[...] = returned[2] * tap_scale

    @pl.when(alone)
    def _():
        block_copy(outgoing.at[:, many, :], out_send, out_recv).wait_send()
        block_copy(results.at[:, most, :], back_send, back_recv).wait_send()

    @pl.when(paired)
    def _():
        block_copy(outgoing, out_send, out_recv).wait_send()

    @pl.when(jnp.logical_and(owner, paired))
    def _():
        block_copy(results, back_send, back_recv).wait_send()


def store_kernel(*refs):
    copies = [
        pltpu.make_async_copy(source, target, refs[-1].at[at])
        for at, (source, target) in enumerate(zip(refs[:3], refs[3:6]))
    ]
    for copy in copies:
        copy.start()
    for copy in copies:
        copy.wait()


def local(devices, streams, filter_raw, grad_output):
    channels, lanes = filter_raw.shape
    tap_scale = 1.0 / math.sqrt(lanes * devices)
    tables = [jnp.asarray(table) for table in make_tables(devices, lanes)]
    vmem = pl.BlockSpec(memory_space=pltpu.VMEM)
    anywhere = pl.BlockSpec(memory_space=pl.ANY)
    inputs = (streams, filter_raw, grad_output)
    operands = [pltpu.with_memory_space_constraint(x, pltpu.HBM) for x in (*inputs, *tables)]
    results = pl.pallas_call(
        functools.partial(kernel, devices, tap_scale),
        out_shape=(
            jax.ShapeDtypeStruct((channels, lanes), jnp.bfloat16),
            jax.ShapeDtypeStruct((3, channels, lanes), jnp.bfloat16),
            jax.ShapeDtypeStruct((channels, lanes), jnp.float32),
        ),
        in_specs=[anywhere] * len(operands),
        out_specs=(vmem, vmem, vmem),
        scratch_shapes=[
            pltpu.VMEM((3, channels, lanes), jnp.float32),
            pltpu.VMEM((3, devices, lanes), jnp.float32),
            pltpu.VMEM((3, devices, lanes), jnp.float32),
            pltpu.VMEM((3, channels, lanes), jnp.float32),
        ]
        + [pltpu.VMEM(table.shape, table.dtype) for table in tables]
        + [pltpu.VMEM(x.shape, x.dtype) for x in inputs]
        + [pltpu.SemaphoreType.DMA((3,)), pltpu.SemaphoreType.DMA((len(tables),))]
        + [pltpu.SemaphoreType.DMA] * 5,
        compiler_params=pltpu.CompilerParams(
            collective_id=0, has_side_effects=True, vmem_limit_bytes=32 << 20
        ),
    )(*operands)
    results = [pltpu.with_memory_space_constraint(x, pltpu.VMEM) for x in results]
    shapes = tuple(jax.ShapeDtypeStruct(x.shape, x.dtype) for x in results)
    return pl.pallas_call(
        store_kernel,
        out_shape=shapes,
        in_specs=[anywhere] * 3,
        out_specs=[anywhere] * 3,
        scratch_shapes=[pltpu.SemaphoreType.DMA((3,))],
        compiler_params=pltpu.CompilerParams(vmem_limit_bytes=8 << 20),
    )(*results)


def solution(mesh):
    devices = mesh.shape["ctx"]
    in_specs = (P(None, "tp", "ctx"), P("tp", "ctx"), P("tp", "ctx"))
    out_specs = (P("tp", "ctx"), P(None, "tp", "ctx"), P("tp", "ctx"))

    def program(streams, filter_raw, grad_output):
        return local(devices, streams, filter_raw, grad_output)

    return jax.shard_map(
        program, mesh=mesh, in_specs=in_specs, out_specs=out_specs, check_vma=False
    )
```

```python
import functools
import math

import jax
import jax.numpy as jnp
import numpy as np
from jax import lax
from jax.experimental import pallas as pl
from jax.experimental.pallas import tpu as pltpu
from jax.sharding import PartitionSpec as P

MESH = pl.DeviceIdType.MESH
ACROSS = 4
FIRST = 4


def split_table(table):
    high = table.astype(jnp.bfloat16)
    low = (table - high.astype(np.float64)).astype(jnp.bfloat16)
    return high, low


def make_tables(rows, lanes):
    length = 2 * rows * lanes
    place = np.arange(rows, dtype=np.int64)
    twice = 2 * np.arange(rows, dtype=np.int64) + 1
    column = np.arange(lanes, dtype=np.int64)
    angle = 2.0 * np.pi / (4 * rows) * (twice[:, None] * place[None, :] % (4 * rows))
    outer = np.concatenate([np.cos(angle), -np.sin(angle)], axis=0)
    angle = 2.0 * np.pi / lanes * (column[:, None] * column[None, :] % lanes)
    cosine, sine = np.cos(angle), np.sin(angle)
    inner = np.block([[cosine, -sine], [sine, cosine]])
    angle = 2.0 * np.pi / (2 * length) * (twice[:, None] * column[None, :] % (2 * length))
    twist = np.stack([np.cos(angle), np.sin(angle)]).astype(np.float32)
    scale = 2.0 / length
    tables = []
    for table in (outer, inner, inner.T, outer.T * scale):
        tables.extend(split_table(table))
    return tables + [twist]


def split_value(value):
    high = value.astype(jnp.bfloat16)
    low = (value - high.astype(jnp.float32)).astype(jnp.bfloat16)
    return high, low


def dot(left, right):
    return jnp.dot(left, right, preferred_element_type=jnp.float32)


def table_times(high, low, value):
    value_high, value_low = split_value(value)
    return dot(high[...], value_high) + (dot(high[...], value_low) + dot(low[...], value_high))


def times_table(value, high, low):
    value_high, value_low = split_value(value)
    return dot(value_high, high[...]) + (dot(value_low, high[...]) + dot(value_high, low[...]))


def convolve(signal, tables, rows_count, lanes):
    outer_high, outer_low, inner_high, inner_low = tables[:4]
    back_high, back_low, final_high, final_low, twist = tables[4:]
    cosine, sine = twist[0], twist[1]
    rows = table_times(outer_high, outer_low, signal)
    spectra = []
    for at in range(3):
        real = rows[:rows_count, at * lanes : (at + 1) * lanes]
        imag = rows[rows_count:, at * lanes : (at + 1) * lanes]
        turned = jnp.concatenate([real * cosine + imag * sine, imag * cosine - real * sine], axis=1)
        both = times_table(turned, inner_high, inner_low)
        spectra.append((both[:, :lanes], both[:, lanes:]))
    (gated_r, gated_i), (taps_r, taps_i), (grad_r, grad_i) = spectra
    products = (
        (gated_r * taps_r - gated_i * taps_i, gated_r * taps_i + gated_i * taps_r),
        (grad_r * taps_r + grad_i * taps_i, grad_i * taps_r - grad_r * taps_i),
        (grad_r * gated_r + grad_i * gated_i, grad_i * gated_r - grad_r * gated_i),
    )
    columns = []
    for real, imag in products:
        both = times_table(jnp.concatenate([real, imag], axis=1), back_high, back_low)
        real, imag = both[:, :lanes], both[:, lanes:]
        columns.append(
            jnp.concatenate([real * cosine - imag * sine, imag * cosine + real * sine], axis=0)
        )
    return table_times(final_high, final_low, jnp.concatenate(columns, axis=1))


def kernel(devices, tap_scale, streams_hbm, filter_hbm, grad_hbm, *refs):
    tables_hbm = refs[:9]
    mixed_ref, grads_ref, taps_ref = refs[9:12]
    outgoing, arrived, results, returned = refs[12:16]
    tables = refs[16:25]
    streams_ref, filter_ref, grad_ref = refs[25:28]
    input_sem, table_sem, out_send, out_recv, back_send, back_recv, self_sem = refs[28:]
    channels, lanes = filter_ref.shape
    me = lax.axis_index("ctx")
    tp = lax.axis_index("tp")
    barrier = pltpu.get_barrier_semaphore()

    plane = ACROSS * 2
    planes = devices // plane
    zed = me // plane
    side = lax.rem(me, plane) // ACROSS
    why = lax.rem(me, ACROSS)
    whys = [lax.rem(why + turn, ACROSS) for turn in range(ACROSS)]
    sides = [side * ACROSS, (1 - side) * ACROSS]
    far_turns = (2, 1, 3, 0)
    spots = [sides[flip] + whys[turn] for turn in far_turns for flip in (1, 0)]

    core = lax.rem(tp, 2)
    low = tp // 2
    keeper = lax.select(core == 0, 3 - 2 * low, tp)
    served = lax.select(side == low, tp, 2 - 2 * low)
    home = zed * ACROSS + why
    owner = core == 1
    alone = jnp.logical_and(owner, side == low)
    paired = jnp.logical_not(alone)
    mates = [whys[turn] for turn in far_turns]

    def plane_of(step):
        half = planes // 2
        back = (step + 1) // 2
        jump = lax.select(lax.rem(step, 2) == 0, half - back, half + back)
        return lax.rem(zed + jump, planes) * plane

    @pl.when(owner)
    def _():
        def greet(peer):
            pl.semaphore_signal(barrier, inc=1, device_id=(peer, served), device_id_type=MESH)

        @pl.loop(0, planes - 1)
        def _(step):
            start = plane_of(step)
            for spot in spots:
                greet(start + spot)

        for spot in spots[:-1]:
            greet(zed * plane + spot)

        @pl.when(paired)
        def _():
            greet(me)

    inputs = [
        pltpu.make_async_copy(source, target, input_sem.at[at])
        for at, (source, target) in enumerate(
            zip((streams_hbm, filter_hbm, grad_hbm), (streams_ref, filter_ref, grad_ref))
        )
    ]
    loads = [
        pltpu.make_async_copy(source, target, table_sem.at[at])
        for at, (source, target) in enumerate(zip(tables_hbm, tables))
    ]
    for load in inputs:
        load.start()

    @pl.when(owner)
    def _():
        for load in loads:
            load.start()

    for load in inputs:
        load.wait()
    query = streams_ref[0].astype(jnp.float32)
    key = streams_ref[1].astype(jnp.float32)
    value = streams_ref[2].astype(jnp.float32)
    upstream = grad_ref[...].astype(jnp.float32)
    outgoing[0] = key * value
    outgoing[1] = filter_ref[...] * tap_scale
    outgoing[2] = query * upstream
    @pl.when(alone)
    def _():
        pl.semaphore_wait(barrier, channels - 1)

    @pl.when(paired)
    def _():
        pl.semaphore_wait(barrier, channels)

    def send_out(number):
        pltpu.make_async_remote_copy(
            src_ref=outgoing.at[:, pl.ds(number, 1), :],
            dst_ref=arrived.at[:, pl.ds(me, 1), :],
            send_sem=out_send,
            recv_sem=out_recv,
            device_id=(number // ACROSS * plane + low * ACROSS + lax.rem(number, ACROSS), keeper),
            device_id_type=MESH,
        ).start()

    def send_back(target):
        pltpu.make_async_remote_copy(
            src_ref=results.at[:, pl.ds(target, 1), :],
            dst_ref=returned.at[:, pl.ds(home, 1), :],
            send_sem=back_send,
            recv_sem=back_recv,
            device_id=(target, served),
            device_id_type=MESH,
        ).start()

    def block_copy(block, send_sem, recv_sem):
        return pltpu.make_async_remote_copy(
            src_ref=block,
            dst_ref=block,
            send_sem=send_sem,
            recv_sem=recv_sem,
            device_id=(me, lax.rem(tp + 1, 4)),
            device_id_type=MESH,
        )

    def keep(source, target):
        copy = pltpu.make_async_copy(source, target, self_sem)
        copy.start()
        copy.wait()

    mine = pl.ds(me, 1)
    housed = pl.ds(home, 1)
    most = pl.ds(0, devices - 1)
    many = pl.ds(0, channels - 1)

    @pl.loop(0, planes - 1)
    def _(step):
        start = plane_of(step) // 2
        for mate in mates:
            send_out(start + mate)

    for mate in mates[:-1]:
        send_out(zed * ACROSS + mate)

    @pl.when(paired)
    def _():
        send_out(home)

    @pl.when(owner)
    def _():
        for load in loads:
            load.wait()

        @pl.when(alone)
        def _():
            keep(outgoing.at[:, housed, :], arrived.at[:, mine, :])
            block_copy(arrived.at[:, most, :], out_send, out_recv).wait_recv()

        @pl.when(paired)
        def _():
            block_copy(arrived, out_send, out_recv).wait_recv()

        signal = jnp.concatenate(
            [arrived[at] for at in range(3)], axis=1
        )
        final = convolve(signal, tables, devices, lanes)
        for at in range(3):
            results[at] = final[:, at * lanes : (at + 1) * lanes]

        def back_plane(start):
            for spot in spots:
                send_back(start + spot)

        @pl.loop(0, FIRST)
        def _(step):
            turn = lax.select(jnp.logical_and(alone, low == 1), 0, zed)
            number = lax.rem(turn + step, FIRST)

            @pl.when(number != zed)
            def _():
                back_plane(number * plane)

        @pl.loop(0, planes - 1)
        def _(step):
            start = plane_of(step)

            @pl.when(start >= FIRST * plane)
            def _():
                back_plane(start)

        for spot in spots[:-1]:
            send_back(zed * plane + spot)

        @pl.when(paired)
        def _():
            send_back(me)

    @pl.when(alone)
    def _():
        keep(results.at[:, mine, :], returned.at[:, housed, :])
        block_copy(returned.at[:, many, :], back_send, back_recv).wait_recv()

    @pl.when(paired)
    def _():
        block_copy(returned, back_send, back_recv).wait_recv()

    long_conv = returned[0]
    grad_gated = returned[1]
    mixed_ref[...] = (streams_ref[0].astype(jnp.float32) * long_conv).astype(jnp.bfloat16)
    grads_ref[0] = (grad_ref[...].astype(jnp.float32) * long_conv).astype(jnp.bfloat16)
    grads_ref[1] = (grad_gated * streams_ref[2].astype(jnp.float32)).astype(jnp.bfloat16)
    grads_ref[2] = (grad_gated * streams_ref[1].astype(jnp.float32)).astype(jnp.bfloat16)
    taps_ref[...] = returned[2] * tap_scale

    @pl.when(alone)
    def _():
        block_copy(outgoing.at[:, many, :], out_send, out_recv).wait_send()
        block_copy(results.at[:, most, :], back_send, back_recv).wait_send()

    @pl.when(paired)
    def _():
        block_copy(outgoing, out_send, out_recv).wait_send()

    @pl.when(jnp.logical_and(owner, paired))
    def _():
        block_copy(results, back_send, back_recv).wait_send()


def store_kernel(*refs):
    copies = [
        pltpu.make_async_copy(source, target, refs[-1].at[at])
        for at, (source, target) in enumerate(zip(refs[:3], refs[3:6]))
    ]
    for copy in copies:
        copy.start()
    for copy in copies:
        copy.wait()


def local(devices, streams, filter_raw, grad_output):
    channels, lanes = filter_raw.shape
    tap_scale = 1.0 / math.sqrt(lanes * devices)
    tables = [jnp.asarray(table) for table in make_tables(devices, lanes)]
    vmem = pl.BlockSpec(memory_space=pltpu.VMEM)
    anywhere = pl.BlockSpec(memory_space=pl.ANY)
    inputs = (streams, filter_raw, grad_output)
    operands = [pltpu.with_memory_space_constraint(x, pltpu.HBM) for x in (*inputs, *tables)]
    results = pl.pallas_call(
        functools.partial(kernel, devices, tap_scale),
        out_shape=(
            jax.ShapeDtypeStruct((channels, lanes), jnp.bfloat16),
            jax.ShapeDtypeStruct((3, channels, lanes), jnp.bfloat16),
            jax.ShapeDtypeStruct((channels, lanes), jnp.float32),
        ),
        in_specs=[anywhere] * len(operands),
        out_specs=(vmem, vmem, vmem),
        scratch_shapes=[
            pltpu.VMEM((3, channels, lanes), jnp.float32),
            pltpu.VMEM((3, devices, lanes), jnp.float32),
            pltpu.VMEM((3, devices, lanes), jnp.float32),
            pltpu.VMEM((3, channels, lanes), jnp.float32),
        ]
        + [pltpu.VMEM(table.shape, table.dtype) for table in tables]
        + [pltpu.VMEM(x.shape, x.dtype) for x in inputs]
        + [pltpu.SemaphoreType.DMA((3,)), pltpu.SemaphoreType.DMA((len(tables),))]
        + [pltpu.SemaphoreType.DMA] * 5,
        compiler_params=pltpu.CompilerParams(
            collective_id=0, has_side_effects=True, vmem_limit_bytes=32 << 20
        ),
    )(*operands)
    results = [pltpu.with_memory_space_constraint(x, pltpu.VMEM) for x in results]
    shapes = tuple(jax.ShapeDtypeStruct(x.shape, x.dtype) for x in results)
    return pl.pallas_call(
        store_kernel,
        out_shape=shapes,
        in_specs=[anywhere] * 3,
        out_specs=[anywhere] * 3,
        scratch_shapes=[pltpu.SemaphoreType.DMA((3,))],
        compiler_params=pltpu.CompilerParams(vmem_limit_bytes=8 << 20),
    )(*results)


def solution(mesh):
    devices = mesh.shape["ctx"]
    in_specs = (P(None, "tp", "ctx"), P("tp", "ctx"), P("tp", "ctx"))
    out_specs = (P("tp", "ctx"), P(None, "tp", "ctx"), P("tp", "ctx"))

    def program(streams, filter_raw, grad_output):
        return local(devices, streams, filter_raw, grad_output)

    return jax.shard_map(
        program, mesh=mesh, in_specs=in_specs, out_specs=out_specs, check_vma=False
    )
```

```python
import functools
import math

import jax
import jax.numpy as jnp
import numpy as np
from jax import lax
from jax.experimental import pallas as pl
from jax.experimental.pallas import tpu as pltpu
from jax.sharding import PartitionSpec as P

MESH = pl.DeviceIdType.MESH
ACROSS = 4
FIRST = 3


def split_table(table):
    high = table.astype(jnp.bfloat16)
    low = (table - high.astype(np.float64)).astype(jnp.bfloat16)
    return high, low


def make_tables(rows, lanes):
    length = 2 * rows * lanes
    place = np.arange(rows, dtype=np.int64)
    twice = 2 * np.arange(rows, dtype=np.int64) + 1
    column = np.arange(lanes, dtype=np.int64)
    angle = 2.0 * np.pi / (4 * rows) * (twice[:, None] * place[None, :] % (4 * rows))
    outer = np.concatenate([np.cos(angle), -np.sin(angle)], axis=0)
    angle = 2.0 * np.pi / lanes * (column[:, None] * column[None, :] % lanes)
    cosine, sine = np.cos(angle), np.sin(angle)
    inner = np.block([[cosine, -sine], [sine, cosine]])
    angle = 2.0 * np.pi / (2 * length) * (twice[:, None] * column[None, :] % (2 * length))
    twist = np.stack([np.cos(angle), np.sin(angle)]).astype(np.float32)
    scale = 2.0 / length
    tables = []
    for table in (outer, inner, inner.T, outer.T * scale):
        tables.extend(split_table(table))
    return tables + [twist]


def split_value(value):
    high = value.astype(jnp.bfloat16)
    low = (value - high.astype(jnp.float32)).astype(jnp.bfloat16)
    return high, low


def dot(left, right):
    return jnp.dot(left, right, preferred_element_type=jnp.float32)


def table_times(high, low, value):
    value_high, value_low = split_value(value)
    return dot(high[...], value_high) + (dot(high[...], value_low) + dot(low[...], value_high))


def times_table(value, high, low):
    value_high, value_low = split_value(value)
    return dot(value_high, high[...]) + (dot(value_low, high[...]) + dot(value_high, low[...]))


def convolve(signal, tables, rows_count, lanes):
    outer_high, outer_low, inner_high, inner_low = tables[:4]
    back_high, back_low, final_high, final_low, twist = tables[4:]
    cosine, sine = twist[0], twist[1]
    rows = table_times(outer_high, outer_low, signal)
    spectra = []
    for at in range(3):
        real = rows[:rows_count, at * lanes : (at + 1) * lanes]
        imag = rows[rows_count:, at * lanes : (at + 1) * lanes]
        turned = jnp.concatenate([real * cosine + imag * sine, imag * cosine - real * sine], axis=1)
        both = times_table(turned, inner_high, inner_low)
        spectra.append((both[:, :lanes], both[:, lanes:]))
    (gated_r, gated_i), (taps_r, taps_i), (grad_r, grad_i) = spectra
    products = (
        (gated_r * taps_r - gated_i * taps_i, gated_r * taps_i + gated_i * taps_r),
        (grad_r * taps_r + grad_i * taps_i, grad_i * taps_r - grad_r * taps_i),
        (grad_r * gated_r + grad_i * gated_i, grad_i * gated_r - grad_r * gated_i),
    )
    columns = []
    for real, imag in products:
        both = times_table(jnp.concatenate([real, imag], axis=1), back_high, back_low)
        real, imag = both[:, :lanes], both[:, lanes:]
        columns.append(
            jnp.concatenate([real * cosine - imag * sine, imag * cosine + real * sine], axis=0)
        )
    return table_times(final_high, final_low, jnp.concatenate(columns, axis=1))


def kernel(devices, tap_scale, streams_hbm, filter_hbm, grad_hbm, *refs):
    tables_hbm = refs[:9]
    mixed_ref, grads_ref, taps_ref = refs[9:12]
    outgoing, arrived, results, returned = refs[12:16]
    tables = refs[16:25]
    streams_ref, filter_ref, grad_ref = refs[25:28]
    input_sem, table_sem, out_send, out_recv, back_send, back_recv, self_sem = refs[28:]
    channels, lanes = filter_ref.shape
    me = lax.axis_index("ctx")
    tp = lax.axis_index("tp")
    barrier = pltpu.get_barrier_semaphore()

    plane = ACROSS * 2
    planes = devices // plane
    zed = me // plane
    side = lax.rem(me, plane) // ACROSS
    why = lax.rem(me, ACROSS)
    whys = [lax.rem(why + turn, ACROSS) for turn in range(ACROSS)]
    sides = [side * ACROSS, (1 - side) * ACROSS]
    far_turns = (2, 1, 3, 0)
    spots = [sides[flip] + whys[turn] for turn in far_turns for flip in (1, 0)]

    core = lax.rem(tp, 2)
    low = tp // 2
    keeper = lax.select(core == 0, 3 - 2 * low, tp)
    served = lax.select(side == low, tp, 2 - 2 * low)
    home = zed * ACROSS + why
    owner = core == 1
    alone = jnp.logical_and(owner, side == low)
    paired = jnp.logical_not(alone)
    mates = [whys[turn] for turn in far_turns]

    def plane_of(step):
        half = planes // 2
        back = (step + 1) // 2
        jump = lax.select(lax.rem(step, 2) == 0, half - back, half + back)
        return lax.rem(zed + jump, planes) * plane

    @pl.when(owner)
    def _():
        def greet(peer):
            pl.semaphore_signal(barrier, inc=1, device_id=(peer, served), device_id_type=MESH)

        @pl.loop(0, planes - 1)
        def _(step):
            start = plane_of(step)
            for spot in spots:
                greet(start + spot)

        for spot in spots[:-1]:
            greet(zed * plane + spot)

        @pl.when(paired)
        def _():
            greet(me)

    inputs = [
        pltpu.make_async_copy(source, target, input_sem.at[at])
        for at, (source, target) in enumerate(
            zip((streams_hbm, filter_hbm, grad_hbm), (streams_ref, filter_ref, grad_ref))
        )
    ]
    loads = [
        pltpu.make_async_copy(source, target, table_sem.at[at])
        for at, (source, target) in enumerate(zip(tables_hbm, tables))
    ]
    for load in inputs + loads:
        load.start()
    for load in inputs:
        load.wait()
    query = streams_ref[0].astype(jnp.float32)
    key = streams_ref[1].astype(jnp.float32)
    value = streams_ref[2].astype(jnp.float32)
    upstream = grad_ref[...].astype(jnp.float32)
    outgoing[0] = key * value
    outgoing[1] = filter_ref[...] * tap_scale
    outgoing[2] = query * upstream
    for load in loads:
        load.wait()

    @pl.when(alone)
    def _():
        pl.semaphore_wait(barrier, channels - 1)

    @pl.when(paired)
    def _():
        pl.semaphore_wait(barrier, channels)

    def send_out(number):
        pltpu.make_async_remote_copy(
            src_ref=outgoing.at[:, pl.ds(number, 1), :],
            dst_ref=arrived.at[:, pl.ds(me, 1), :],
            send_sem=out_send,
            recv_sem=out_recv,
            device_id=(number // ACROSS * plane + low * ACROSS + lax.rem(number, ACROSS), keeper),
            device_id_type=MESH,
        ).start()

    def send_back(target):
        pltpu.make_async_remote_copy(
            src_ref=results.at[:, pl.ds(target, 1), :],
            dst_ref=returned.at[:, pl.ds(home, 1), :],
            send_sem=back_send,
            recv_sem=back_recv,
            device_id=(target, served),
            device_id_type=MESH,
        ).start()

    def block_copy(block, send_sem, recv_sem):
        return pltpu.make_async_remote_copy(
            src_ref=block,
            dst_ref=block,
            send_sem=send_sem,
            recv_sem=recv_sem,
            device_id=(me, lax.rem(tp + 1, 4)),
            device_id_type=MESH,
        )

    def keep(source, target):
        copy = pltpu.make_async_copy(source, target, self_sem)
        copy.start()
        copy.wait()

    mine = pl.ds(me, 1)
    housed = pl.ds(home, 1)
    most = pl.ds(0, devices - 1)
    many = pl.ds(0, channels - 1)

    @pl.loop(0, planes - 1)
    def _(step):
        start = plane_of(step) // 2
        for mate in mates:
            send_out(start + mate)

    for mate in mates[:-1]:
        send_out(zed * ACROSS + mate)

    @pl.when(paired)
    def _():
        send_out(home)

    @pl.when(owner)
    def _():
        @pl.when(alone)
        def _():
            keep(outgoing.at[:, housed, :], arrived.at[:, mine, :])
            block_copy(arrived.at[:, most, :], out_send, out_recv).wait_recv()

        @pl.when(paired)
        def _():
            block_copy(arrived, out_send, out_recv).wait_recv()

        signal = jnp.concatenate(
            [arrived[at] for at in range(3)], axis=1
        )
        final = convolve(signal, tables, devices, lanes)
        for at in range(3):
            results[at] = final[:, at * lanes : (at + 1) * lanes]

        def back_plane(start):
            for spot in spots:
                send_back(start + spot)

        @pl.loop(0, FIRST)
        def _(step):
            turn = lax.select(low == 1, 0, zed)
            number = lax.rem(turn + step, FIRST)

            @pl.when(number != zed)
            def _():
                back_plane(number * plane)

        @pl.loop(0, planes - 1)
        def _(step):
            start = plane_of(step)

            @pl.when(start >= FIRST * plane)
            def _():
                back_plane(start)

        for spot in spots[:-1]:
            send_back(zed * plane + spot)

        @pl.when(paired)
        def _():
            send_back(me)

    @pl.when(alone)
    def _():
        keep(results.at[:, mine, :], returned.at[:, housed, :])
        block_copy(returned.at[:, many, :], back_send, back_recv).wait_recv()

    @pl.when(paired)
    def _():
        block_copy(returned, back_send, back_recv).wait_recv()

    long_conv = returned[0]
    grad_gated = returned[1]
    mixed_ref[...] = (streams_ref[0].astype(jnp.float32) * long_conv).astype(jnp.bfloat16)
    grads_ref[0] = (grad_ref[...].astype(jnp.float32) * long_conv).astype(jnp.bfloat16)
    grads_ref[1] = (grad_gated * streams_ref[2].astype(jnp.float32)).astype(jnp.bfloat16)
    grads_ref[2] = (grad_gated * streams_ref[1].astype(jnp.float32)).astype(jnp.bfloat16)
    taps_ref[...] = returned[2] * tap_scale

    @pl.when(alone)
    def _():
        block_copy(outgoing.at[:, many, :], out_send, out_recv).wait_send()
        block_copy(results.at[:, most, :], back_send, back_recv).wait_send()

    @pl.when(paired)
    def _():
        block_copy(outgoing, out_send, out_recv).wait_send()

    @pl.when(jnp.logical_and(owner, paired))
    def _():
        block_copy(results, back_send, back_recv).wait_send()


def store_kernel(*refs):
    copies = [
        pltpu.make_async_copy(source, target, refs[-1].at[at])
        for at, (source, target) in enumerate(zip(refs[:3], refs[3:6]))
    ]
    for copy in copies:
        copy.start()
    for copy in copies:
        copy.wait()


def local(devices, streams, filter_raw, grad_output):
    channels, lanes = filter_raw.shape
    tap_scale = 1.0 / math.sqrt(lanes * devices)
    tables = [jnp.asarray(table) for table in make_tables(devices, lanes)]
    vmem = pl.BlockSpec(memory_space=pltpu.VMEM)
    anywhere = pl.BlockSpec(memory_space=pl.ANY)
    inputs = (streams, filter_raw, grad_output)
    operands = [pltpu.with_memory_space_constraint(x, pltpu.HBM) for x in (*inputs, *tables)]
    results = pl.pallas_call(
        functools.partial(kernel, devices, tap_scale),
        out_shape=(
            jax.ShapeDtypeStruct((channels, lanes), jnp.bfloat16),
            jax.ShapeDtypeStruct((3, channels, lanes), jnp.bfloat16),
            jax.ShapeDtypeStruct((channels, lanes), jnp.float32),
        ),
        in_specs=[anywhere] * len(operands),
        out_specs=(vmem, vmem, vmem),
        scratch_shapes=[
            pltpu.VMEM((3, channels, lanes), jnp.float32),
            pltpu.VMEM((3, devices, lanes), jnp.float32),
            pltpu.VMEM((3, devices, lanes), jnp.float32),
            pltpu.VMEM((3, channels, lanes), jnp.float32),
        ]
        + [pltpu.VMEM(table.shape, table.dtype) for table in tables]
        + [pltpu.VMEM(x.shape, x.dtype) for x in inputs]
        + [pltpu.SemaphoreType.DMA((3,)), pltpu.SemaphoreType.DMA((len(tables),))]
        + [pltpu.SemaphoreType.DMA] * 5,
        compiler_params=pltpu.CompilerParams(
            collective_id=0, has_side_effects=True, vmem_limit_bytes=32 << 20
        ),
    )(*operands)
    results = [pltpu.with_memory_space_constraint(x, pltpu.VMEM) for x in results]
    shapes = tuple(jax.ShapeDtypeStruct(x.shape, x.dtype) for x in results)
    return pl.pallas_call(
        store_kernel,
        out_shape=shapes,
        in_specs=[anywhere] * 3,
        out_specs=[anywhere] * 3,
        scratch_shapes=[pltpu.SemaphoreType.DMA((3,))],
        compiler_params=pltpu.CompilerParams(vmem_limit_bytes=8 << 20),
    )(*results)


def solution(mesh):
    devices = mesh.shape["ctx"]
    in_specs = (P(None, "tp", "ctx"), P("tp", "ctx"), P("tp", "ctx"))
    out_specs = (P("tp", "ctx"), P(None, "tp", "ctx"), P("tp", "ctx"))

    def program(streams, filter_raw, grad_output):
        return local(devices, streams, filter_raw, grad_output)

    return jax.shard_map(
        program, mesh=mesh, in_specs=in_specs, out_specs=out_specs, check_vma=False
    )
```
